256 devices in a mesh: src: 8 (over x, y_hi), tgt: 32 (over z, y_lo, core).
Axes of the slice: x: 4, y: 4 (y_hi: 2, y_lo: 2; y = y_hi * 2 + y_lo), z: 8, core: 2. Of those that a mesh axis runs over, the one named last changes fastest.
Arguments:
- source_feats: bfloat16 [1, 32, 32, 1024], P(None, 'src', None, 'tgt'), may hold values from -200 to 200
- target_feats: bfloat16 [1, 128, 32, 1024], P(None, 'tgt', None, 'src'), may hold values from -200 to 200
- conv_one: bfloat16 [3, 3, 3, 3, 1, 16], replicated, may hold values from -1 to 1
- bias_one: float32 [16], replicated, may hold values from -1.5 to 1.5
- conv_two: bfloat16 [3, 3, 3, 3, 16, 16], replicated, may hold values from -0.25 to 0.25
- bias_two: float32 [16], replicated, may hold values from -1.5 to 1.5
- conv_three: bfloat16 [3, 3, 3, 3, 16, 1], replicated, may hold values from -0.25 to 0.25
- bias_three: float32 [1], replicated, may hold values from -1.5 to 1.5
Outputs:
- scores: bfloat16 [1, 32, 128, 32, 32], P(None, 'src', 'tgt')
The draws below stay inside these ranges and needn't reach their ends.
All inputs are finite; a program needn't handle non-finite values.
Results may differ from the reference program's by a relative error of at most 0.0049.
The reference program's roundings to bfloat16 on the way count: a program that leaves them out, or rounds other values in their place, can miss the bound.
Values may be sent and summed in bfloat16 or wider, within the bound.
A program may use at most 256 MiB of HBM per device.

```python
import jax
import jax.numpy as jnp
from jax import lax

C = 1024
CH = 16
WA = 32
WB = 32
PAIRS = 1
HA = 32
HB = 128


def feature_draw(key, rows, cols, salt):
    protos = jax.random.normal(jax.random.fold_in(key, 7), (8, C), jnp.float32)
    own_key = jax.random.fold_in(key, salt)
    labels = jax.random.randint(jax.random.fold_in(own_key, 1), (PAIRS, rows, cols), 0, 8)
    onehot = (labels[..., None] == jnp.arange(8, dtype=jnp.int32)).astype(jnp.float32)
    mixed = jnp.einsum('pijk,kc->pijc', onehot, protos)
    noise = jax.random.normal(jax.random.fold_in(own_key, 2), (PAIRS, rows, cols, C), jnp.float32)
    channel_scale = 10.0 ** (jnp.arange(C, dtype=jnp.float32) / C)
    values = (1.2 * mixed + noise) * channel_scale
    return jnp.clip(values, -200.0, 200.0).astype(jnp.bfloat16)


def draw_source_feats(key, part):
    return feature_draw(key, HA, WA, 11)


def draw_target_feats(key, part):
    return feature_draw(key, HB, WB, 23)


def centred(stream_key, dims, spread, bound, held_as=jnp.bfloat16):
    drawn = spread * jax.random.normal(stream_key, dims, jnp.float32)
    return jnp.clip(drawn, min=-bound, max=bound).astype(held_as)


def setup_inputs(seed: int = 0) -> dict:
    arg_keys = jax.random.split(jax.random.key(seed), 9)
    return {
        "source_feats": draw_source_feats(jax.random.fold_in(arg_keys[8], 71), 0),
        "target_feats": draw_target_feats(jax.random.fold_in(arg_keys[8], 71), 0),
        "conv_one": centred(arg_keys[2], (3, 3, 3, 3, 1, CH), 40 ** -0.5, 1.0),
        "bias_one": centred(arg_keys[3], (CH,), 0.3, 1.5, jnp.float32),
        "conv_two": centred(arg_keys[4], (3, 3, 3, 3, CH, CH), (40 * CH) ** -0.5, 0.25),
        "bias_two": centred(arg_keys[5], (CH,), 0.3, 1.5, jnp.float32),
        "conv_three": centred(arg_keys[6], (3, 3, 3, 3, CH, 1), (40 * CH) ** -0.5, 0.25),
        "bias_three": centred(arg_keys[7], (1,), 0.5, 1.5, jnp.float32),
    }


epsilon = 1e-06

def normalize(feats):
    values = feats.astype(jnp.float32)
    squares = lax.optimization_barrier(jnp.sum(values * values, axis=-1, keepdims=True))
    return (values * lax.rsqrt(squares + epsilon)).astype(jnp.bfloat16)

def layer_ref(volume, kernel, biases):
    cout = kernel.shape[-1]
    padded = jnp.pad(volume, ((0, 0), (1, 1), (1, 1), (1, 1), (1, 1)))
    summed = jnp.zeros((cout, HA, WA, HB, WB), jnp.float32)
    for row_step in range(3):
        for col_step in range(3):
            for tgt_step in range(3):
                for lane_step in range(3):
                    piece = padded[:, row_step:row_step + HA, col_step:col_step + WA, tgt_step:tgt_step + HB, lane_step:lane_step + WB]
                    tap = kernel[row_step, col_step, tgt_step, lane_step].astype(jnp.float32)
                    summed = summed + jnp.einsum('aijkl,ab->bijkl', piece.astype(jnp.float32), tap)
    return jax.nn.relu(summed + biases[:, None, None, None, None]).astype(jnp.bfloat16)

def reference(source_feats, target_feats, conv_one, bias_one, conv_two, bias_two, conv_three, bias_three):

    def one_pair(pair):
        source_part, target_part = pair
        left = normalize(source_part).reshape(HA * WA, C)
        right = normalize(target_part).reshape(HB * WB, C)
        volume = jnp.dot(left, right.T, preferred_element_type=jnp.float32).astype(jnp.bfloat16)
        volume = volume.reshape(1, HA, WA, HB, WB)
        volume = layer_ref(volume, conv_one, bias_one)
        volume = layer_ref(volume, conv_two, bias_two)
        volume = layer_ref(volume, conv_three, bias_three)
        return jnp.transpose(volume[0], (0, 2, 1, 3))
    return lax.map(one_pair, (source_feats, target_feats))
```

```python
import functools

import jax
import jax.numpy as jnp
from jax import lax
from jax.experimental import pallas as pl
from jax.experimental.pallas import tpu as pltpu
from jax.sharding import PartitionSpec as P

F32, BF = jnp.float32, jnp.bfloat16

MESH = pl.DeviceIdType.MESH
EPS = 1e-6
SIDES = [(ds, dt) for ds in (-1, 0, 1) for dt in (-1, 0, 1) if ds or dt]


def halo_span(d):
    if d == 0:
        return 0, 4, 3
    return (1, 3, 0) if d > 0 else (0, 3, 7)


def volume_kernel(ns, nt, src_ref, tgt_ref, vol, gs, gt, own, s_send, s_recv, t_send, t_recv, h_send, h_recv):
    s, t = lax.axis_index("src"), lax.axis_index("tgt")
    ch_s, ch_t = src_ref.shape[-1], tgt_ref.shape[-1]

    vol[...] = jnp.zeros_like(vol)
    barrier = pltpu.get_barrier_semaphore()

    def greet(ds, dt):
        pl.semaphore_signal(barrier, inc=1, device_id=(s + ds, t + dt), device_id_type=MESH)

    @pl.loop(1, nt)
    def _(r):
        pl.semaphore_signal(barrier, inc=1, device_id=(s, lax.rem(t + r, nt)), device_id_type=MESH)

    @pl.loop(1, ns)
    def _(r):
        pl.semaphore_signal(barrier, inc=1, device_id=(lax.rem(s + r, ns), t), device_id_type=MESH)

    def there(ds, dt):
        return (s + ds >= 0) & (s + ds < ns) & (t + dt >= 0) & (t + dt < nt)

    count = ns - 1 + nt - 1
    for ds, dt in SIDES:
        if ds and dt:
            count = count + jnp.where(there(ds, dt), 1, 0)

            @pl.when(there(ds, dt))
            def _():
                greet(ds, dt)

    eye = (lax.broadcasted_iota(jnp.int32, (ch_s, ch_s), 0)
           == lax.broadcasted_iota(jnp.int32, (ch_s, ch_s), 1)).astype(BF)
    gs[t] = lax.dot_general(eye, src_ref[...], (((1,), (1,)), ((), ())),
                            preferred_element_type=F32).astype(BF)
    gt[s] = tgt_ref[...]
    pl.semaphore_wait(barrier, count)

    def send_s(r):
        return pltpu.make_async_remote_copy(
            src_ref=gs.at[t], dst_ref=gs.at[t], send_sem=s_send.at[r - 1], recv_sem=s_recv.at[r - 1],
            device_id=(s, lax.rem(t + r, nt)), device_id_type=MESH)

    def got_s(r):
        at = gs.at[lax.rem(t + nt - r, nt)]
        return pltpu.make_async_remote_copy(
            src_ref=at, dst_ref=at, send_sem=s_send.at[r - 1], recv_sem=s_recv.at[r - 1],
            device_id=(s, lax.rem(t + r, nt)), device_id_type=MESH)

    def send_t(r):
        return pltpu.make_async_remote_copy(
            src_ref=tgt_ref, dst_ref=gt.at[s], send_sem=t_send.at[r - 1], recv_sem=t_recv.at[r - 1],
            device_id=(lax.rem(s + r, ns), t), device_id_type=MESH)

    def got_t(r):
        at = gt.at[lax.rem(s + ns - r, ns)]
        return pltpu.make_async_remote_copy(
            src_ref=at, dst_ref=at, send_sem=t_send.at[r - 1], recv_sem=t_recv.at[r - 1],
            device_id=(lax.rem(s + r, ns), t), device_id_type=MESH)

    @pl.loop(1, ns)
    def _(r):
        send_t(r).start()

    @pl.loop(1, nt)
    def _(r):
        send_s(r).start()

    @pl.loop(1, nt)
    def _(r):
        got_s(r).wait_recv()

    sq = None
    for c in range(nt):
        x = gs[c].astype(F32)
        x = x * x
        for q in range(ch_s // 8):
            p = x[8 * q:8 * q + 8]
            sq = p if sq is None else sq + p
    inv_s = lax.rsqrt(jnp.sum(sq, axis=0, keepdims=True) + EPS)

    @pl.loop(1, ns)
    def _(r):
        got_t(r).wait_recv()

    sq = None
    for c in range(ns):
        x = gt[c].astype(F32)
        x = x * x
        sq = x if sq is None else sq + x
    inv_t = lax.rsqrt(jnp.sum(sq, axis=1, keepdims=True) + EPS)

    per = ch_t // ch_s
    acc = jnp.zeros((128, 128), F32)
    for c in range(ns):
        left = jnp.concatenate([gs[c * per + q] for q in range(per)], 0)
        left = (left.astype(F32) * inv_s).astype(BF)
        right = (gt[c].astype(F32) * inv_t).astype(BF)
        acc = acc + jnp.dot(right, left, preferred_element_type=F32)
    v = acc.T
    block = lax.broadcasted_iota(jnp.int32, (8, 128), 1) // 32
    for i in range(4):
        for k in range(4):
            u = None
            for hi in range(4):
                w = v[32 * i + 8 * hi:32 * i + 8 * hi + 8]
                w = pltpu.roll(w, (32 * (hi - k)) % 128, 1) if hi != k else w
                u = w if u is None else jnp.where(block == hi, w, u)
            u = u.astype(BF)
            own[i, k] = u
            vol[3 + i, 3 + k] = u

    def halo(n, ds, dt):
        i0, ni, i1 = halo_span(ds)
        k0, nk, k1 = halo_span(dt)
        return pltpu.make_async_remote_copy(
            src_ref=own.at[pl.ds(i0, ni), pl.ds(k0, nk)], dst_ref=vol.at[pl.ds(i1, ni), pl.ds(k1, nk)],
            send_sem=h_send.at[n], recv_sem=h_recv.at[n], device_id=(s + ds, t + dt), device_id_type=MESH)

    for n, (ds, dt) in enumerate(SIDES):
        @pl.when(there(ds, dt))
        def _():
            halo(n, ds, dt).start()

    for n, (ds, dt) in enumerate(SIDES):
        @pl.when(there(-ds, -dt))
        def _():
            halo(n, ds, dt).wait_recv()

    for n, (ds, dt) in enumerate(SIDES):
        @pl.when(there(ds, dt))
        def _():
            halo(n, ds, dt).wait_send()

    @pl.loop(1, nt)
    def _(r):
        send_s(r).wait_send()

    @pl.loop(1, ns)
    def _(r):
        send_t(r).wait_send()


def volume_call(ns, nt, src, tgt):
    vm = pl.BlockSpec(memory_space=pltpu.VMEM)
    dma = pltpu.SemaphoreType.DMA
    return pl.pallas_call(
        functools.partial(volume_kernel, ns, nt),
        out_shape=jax.ShapeDtypeStruct((10, 10, 8, 128), BF),
        in_specs=[vm, vm], out_specs=vm,
        scratch_shapes=[
            pltpu.VMEM((nt, src.shape[-1], 128), BF),
            pltpu.VMEM((ns, 128, tgt.shape[-1]), BF),
            pltpu.VMEM((4, 4, 8, 128), BF),
            dma((nt - 1,)), dma((nt - 1,)), dma((ns - 1,)), dma((ns - 1,)), dma((8,)), dma((8,)),
        ],
        compiler_params=pltpu.CompilerParams(collective_id=0, has_side_effects=True, vmem_limit_bytes=40 << 20),
    )(src, tgt)


def conv_weights(conv_one, conv_two, conv_three):
    j = jnp.arange(8)[:, None]
    at = jnp.array([0, 1, 2, 3, 4, 5, 6, 7, 8, 90, 90, 90, 90, 90, 90, -1])[None, :]
    hot1 = jnp.stack([(at - j + 1 == b) for b in range(3)]).astype(BF)
    w1 = jnp.einsum("bjJ,abegd->jdaegJ", hot1, conv_one[:, :, :, :, 0, :]).reshape(128, 432)
    w2 = jnp.transpose(conv_two, (3, 5, 0, 2, 1, 4)).reshape(48, 432)
    at3 = (jnp.arange(10) - 1)[None, :]
    hot3 = jnp.stack([(at3 - j + 1 == b) for b in range(3)]).astype(BF)
    w3 = jnp.einsum("bjJ,abegc->gjaeJc", hot3, conv_three[..., 0]).reshape(24, 1440)
    return w1, w2, w3


def rolled(x, by):
    return pltpu.roll(x, by % 128, 1)


def conv_kernel(ns, nt, u_ref, w1_ref, b1_ref, w2_ref, b2_ref, w3_ref, b3_ref, o_ref, z, act1, act2):
    s, t = lax.axis_index("src"), lax.axis_index("tgt")
    lane = lax.broadcasted_iota(jnp.int32, (8, 128), 1)
    row = lax.broadcasted_iota(jnp.int32, (8, 128), 0)
    lane16 = lax.broadcasted_iota(jnp.int32, (16, 128), 1)
    first8, last8 = lane % 32 == 0, lane % 32 == 31
    first, last = lane16 % 32 == 0, lane16 % 32 == 31
    dot = functools.partial(jnp.dot, preferred_element_type=F32)

    @pl.loop(0, 10)
    def _(i):
        for k in range(10):
            u = u_ref[i, k].astype(F32)
            before = jnp.where(lane >= 32, rolled(u, 32), 0.0)
            after = jnp.where(lane < 96, rolled(u, -32), 0.0)
            both = jnp.where(row >= 4, before, after)
            for g in range(3):
                if g == 0:
                    p, q = (jnp.where(first8, 0.0, rolled(v, 1)) for v in (u, both))
                elif g == 1:
                    p, q = u, both
                else:
                    p, q = (jnp.where(last8, 0.0, rolled(v, -1)) for v in (u, both))
                z[i, k, pl.ds(16 * g, 16)] = jnp.concatenate([p, q], 0).astype(BF)

    w1 = w1_ref[...]
    b1 = jnp.broadcast_to(b1_ref[...], (16, 128))

    def put(act, i, k, j, v):
        act[i, k, 1 + j] = v.astype(BF)
        if j == 7:
            act[i, k, 0] = jnp.where(lane16 >= 32, rolled(v, 32), 0.0).astype(BF)
        if j == 0:
            act[i, k, 9] = jnp.where(lane16 < 96, rolled(v, -32), 0.0).astype(BF)

    @pl.loop(0, 8)
    def _(i):
        @pl.loop(0, 4)
        def _(kk):
            cols = []
            for m in range(2):
                cols.append(jnp.concatenate(
                    [z[i + a, 2 * kk + m + e] for a in range(3) for e in range(3)], 0))
            y = dot(w1, jnp.concatenate(cols, 1))
            for m in range(2):
                k = 2 * kk + m
                gi, gk = 4 * s - 2 + i, 4 * t - 2 + k
                ok = (gi >= 0) & (gi < 4 * ns) & (gk >= 0) & (gk < 4 * nt)
                keep = jnp.where(ok, 1.0, 0.0)
                for j in range(8):
                    v = jnp.maximum(y[16 * j:16 * j + 16, 128 * m:128 * m + 128] + b1, 0.0) * keep
                    put(act1, i, k, j, v)

    w2 = w2_ref[...]
    b2 = jnp.broadcast_to(b2_ref[...], (16, 128))

    @pl.loop(0, 6)
    def _(i):
        @pl.loop(0, 6)
        def _(k):
            gi, gk = 4 * s - 1 + i, 4 * t - 1 + k
            ok = (gi >= 0) & (gi < 4 * ns) & (gk >= 0) & (gk < 4 * nt)
            keep = jnp.where(ok, 1.0, 0.0)
            for p in range(4):
                cols = []
                for m in range(2):
                    cols.append(jnp.concatenate(
                        [act1[i + a, k + e, 2 * p + m + b] for a in range(3) for e in range(3) for b in range(3)], 0))
                y = dot(w2, jnp.concatenate(cols, 1))
                for m in range(2):
                    h = slice(128 * m, 128 * m + 128)
                    v = (y[16:32, h] + jnp.where(first, 0.0, rolled(y[0:16, h], 1))
                         + jnp.where(last, 0.0, rolled(y[32:48, h], -1)) + b2)
                    put(act2, i, k, 2 * p + m, jnp.maximum(v, 0.0) * keep)

    w3 = w3_ref[...]
    b3 = b3_ref[0, 0]

    @pl.loop(0, 4)
    def _(i):
        @pl.loop(0, 2)
        def _(kk):
            y = None
            for a in range(3):
                cols = [jnp.concatenate([act2[i + a, 2 * kk + m + e].reshape(160, 128) for e in range(3)], 0)
                        for m in range(2)]
                part = dot(w3[:, 480 * a:480 * a + 480], jnp.concatenate(cols, 1))
                y = part if y is None else y + part
            for m in range(2):
                h = slice(128 * m, 128 * m + 128)
                v = (y[8:16, h] + jnp.where(first8, 0.0, rolled(y[0:8, h], 1))
                     + jnp.where(last8, 0.0, rolled(y[16:24, h], -1)) + b3)
                v = jnp.maximum(v, 0.0)
                o_ref[i, 2 * kk + m] = jnp.concatenate(
                    [v[:, 32 * q:32 * q + 32] for q in range(4)], 0).astype(BF)


def conv_call(ns, nt, u, w1, b1, w2, b2, w3, b3):
    vm = pl.BlockSpec(memory_space=pltpu.VMEM)
    return pl.pallas_call(
        functools.partial(conv_kernel, ns, nt),
        out_shape=jax.ShapeDtypeStruct((4, 4, 32, 32), BF),
        in_specs=[vm, vm, vm, vm, vm, vm, pl.BlockSpec(memory_space=pltpu.SMEM)],
        out_specs=vm,
        scratch_shapes=[
            pltpu.VMEM((10, 10, 48, 128), BF),
            pltpu.VMEM((8, 8, 10, 16, 128), BF),
            pltpu.VMEM((6, 6, 10, 16, 128), BF),
        ],
        compiler_params=pltpu.CompilerParams(vmem_limit_bytes=40 << 20),
    )(u, w1, b1, w2, b2, w3, b3)


def solution(mesh):
    ns, nt = mesh.shape["src"], mesh.shape["tgt"]

    def local(source, target, conv_one, bias_one, conv_two, bias_two, conv_three, bias_three):
        w1, w2, w3 = conv_weights(conv_one, conv_two, conv_three)
        vol = volume_call(ns, nt, source.reshape(128, -1), target.reshape(128, -1))
        out = conv_call(ns, nt, vol, w1, bias_one.reshape(16, 1), w2, bias_two.reshape(16, 1), w3,
                        bias_three.reshape(1, 1))
        return out[None]

    return jax.shard_map(
        local,
        mesh=mesh,
        in_specs=(P(None, "src", None, "tgt"), P(None, "tgt", None, "src")) + (P(),) * 6,
        out_specs=P(None, "src", "tgt", None, None),
        check_vma=False,
    )
```

```python
import functools

import jax
import jax.numpy as jnp
from jax import lax
from jax.experimental import pallas as pl
from jax.experimental.pallas import tpu as pltpu
from jax.sharding import PartitionSpec as P

F32, BF = jnp.float32, jnp.bfloat16

MESH = pl.DeviceIdType.MESH
EPS = 1e-6
SIDES = [(ds, dt) for ds in (-1, 0, 1) for dt in (-1, 0, 1) if ds or dt]
NT = (((1,), (1,)), ((), ()))


def halo_span(d):
    if d == 0:
        return 0, 4, 3
    return (1, 3, 0) if d > 0 else (0, 3, 7)


def iota(shape, dim):
    return lax.broadcasted_iota(jnp.int32, shape, dim)


def hot(mask):
    return jnp.where(mask, 1.0, 0.0).astype(BF)


def make_w1(c1, flat, w1):
    flat[...] = jnp.zeros_like(flat)
    for n in range(27):
        flat[pl.ds(3 * n, 3), pl.ds(0, 16)] = c1[n].astype(F32)
    xt = flat[...].T[0:16, 0:96].astype(BF)
    n = iota((1, 432), 1)
    a, e, g, at = n // 144, (n // 48) % 3, (n // 16) % 3, n % 16
    at = jnp.where(at == 15, -1, jnp.where(at <= 8, at, 100))
    base = a * 27 + e * 3 + g
    r = iota((96, 432), 0)
    for j in range(8):
        b = at - j + 1
        key = jnp.where((b >= 0) & (b < 3), base + 9 * b, -1)
        w1[pl.ds(16 * j, 16)] = jnp.dot(xt, hot(r == key), preferred_element_type=F32).astype(BF)


def make_w2(c2, w2):
    eye = hot(iota((16, 16), 0) == iota((16, 16), 1))
    none = jnp.zeros((16, 16), BF)
    for i in range(2):
        for k in range(2):
            for g in range(3):
                pieces = []
                for up in range(4):
                    for across in range(4):
                        for b in range(3):
                            a, e = up - i, across - k
                            inside = 0 <= a < 3 and 0 <= e < 3
                            pieces.append(c2[((a * 3 + b) * 3 + e) * 3 + g] if inside else none)
                w2[pl.ds(((2 * i + k) * 3 + g) * 16, 16)] = lax.dot_general(
                    eye, jnp.concatenate(pieces, 0), NT, preferred_element_type=F32).astype(BF)


def make_w3(c3, flat, w3):
    flat[...] = jnp.zeros_like(flat)
    for n in range(27):
        flat[pl.ds(3 * n, 3), pl.ds(0, 16)] = c3[n].astype(F32)
    y = flat[pl.ds(0, 96), pl.ds(0, 16)].astype(BF)
    wide = jnp.dot(y, hot(iota((16, 256), 1) % 16 == iota((16, 256), 0)), preferred_element_type=F32).astype(BF)
    m = iota((48, 1), 0)
    b, slot = m // 16, (m % 16) // 4
    g = jnp.where(slot == 0, 1, jnp.where(slot == 1, 0, 2))
    r = iota((48, 96), 1)
    mm, nn = iota((48, 256), 0), iota((48, 256), 1)
    up, across = nn // 64 - (mm // 2) % 2, (nn // 16) % 4 - mm % 2
    total = jnp.zeros((48, 256), F32)
    for a in range(3):
        for e in range(3):
            key = jnp.where(slot < 3, a * 27 + b * 9 + e * 3 + g, -1)
            part = jnp.dot(hot(r == key), wide, preferred_element_type=F32)
            total = total + jnp.where((up == a) & (across == e), part, 0.0)
    w3[...] = total.astype(BF)


def inverse_root(v):
    r = lax.rsqrt(v)
    return r * (1.5 - 0.5 * v * r * r)


def column(row):
    square = jnp.where(iota((16, 16), 0) == iota((16, 16), 1), jnp.broadcast_to(row, (16, 16)), 0.0)
    return jnp.broadcast_to(jnp.sum(square, axis=1, keepdims=True), (16, 128))


def volume_kernel(ns, nt, src_hbm, tgt_hbm, c1_hbm, b1_hbm, c2_hbm, b2_hbm, c3_hbm, b3_ref,
                  vol, w1, w2, w3, bias,
                  src, gs, gt, own, c1, c2, c3, bs, flat1, flat3, load,
                  z_send, z_recv, y_send, y_recv, c_send, c_recv, x_send, x_recv, p_send, p_recv,
                  f_send, f_recv, h_send, h_recv):
    s, t = lax.axis_index("src"), lax.axis_index("tgt")
    nz, nx = nt // 4, ns // 2
    z, y, c = t // 4, (t // 2) % 2, t % 2
    x, h = s // 2, s % 2
    ch_s, ch_t = src.shape[-1], gt.shape[-1]

    fetches = [pltpu.make_async_copy(a, b, load.at[n]) for n, (a, b) in enumerate(
        [(src_hbm, src), (tgt_hbm, gt.at[s]), (c1_hbm, c1), (c2_hbm, c2), (c3_hbm, c3),
         (b1_hbm, bs.at[0]), (b2_hbm, bs.at[1])])]
    for f in fetches:
        f.start()

    vol[...] = jnp.zeros_like(vol)

    def tgt_at(zz, yy, cc):
        return 4 * zz + 2 * yy + cc

    def z_off(r):
        return lax.rem(z + r + nz, nz)

    def x_off(r):
        return lax.rem(x + r + nx, nx)

    def there(ds, dt):
        return (s + ds >= 0) & (s + ds < ns) & (t + dt >= 0) & (t + dt < nt)

    barrier = pltpu.get_barrier_semaphore()
    peers = [(s, tgt_at(z_off(r), y, c)) for r in range(1, nz)]
    peers += [(s, tgt_at(z, 1 - y, c)), (s, tgt_at(z, y, 1 - c))]
    peers += [(2 * x_off(r) + h, t) for r in range(1, nx)] + [(2 * x + 1 - h, t)]
    count = len(peers)
    for p in peers:
        pl.semaphore_signal(barrier, inc=1, device_id=p, device_id_type=MESH)
    for ds, dt in SIDES:
        count = count + jnp.where(there(ds, dt), 1, 0)

        @pl.when(there(ds, dt))
        def _():
            pl.semaphore_signal(barrier, inc=1, device_id=(s + ds, t + dt), device_id_type=MESH)

    fetches[0].wait()
    eye = hot(iota((ch_s, ch_s), 0) == iota((ch_s, ch_s), 1))
    gs[t] = lax.dot_general(eye, src[...], NT, preferred_element_type=F32).astype(BF)
    fetches[1].wait()
    pl.semaphore_wait(barrier, count)

    def remote(ref, sems, n, to):
        return pltpu.make_async_remote_copy(
            src_ref=ref, dst_ref=ref, send_sem=sems[0].at[n], recv_sem=sems[1].at[n],
            device_id=to, device_id_type=MESH)

    zs, ys, cs, xs, ps, fs = ((z_send, z_recv), (y_send, y_recv), (c_send, c_recv), (x_send, x_recv),
                              (p_send, p_recv), (f_send, f_recv))
    mate, twin, partner = (s, tgt_at(z, 1 - y, c)), (s, tgt_at(z, y, 1 - c)), (2 * x + 1 - h, t)

    def z_go(r):
        return remote(gs.at[t], zs, r - 1, (s, tgt_at(z_off(r), y, c)))

    def z_come(r):
        return remote(gs.at[tgt_at(z_off(-r), y, c)], zs, r - 1, mate)

    def y_go(q):
        return remote(gs.at[tgt_at(z_off(-q), y, c)], ys, q, mate)

    def y_come(q):
        return remote(gs.at[tgt_at(z_off(-q), 1 - y, c)], ys, q, mate)

    def c_go(q, w):
        return remote(gs.at[tgt_at(z_off(-q), y if w == 0 else 1 - y, c)], cs, 2 * q + w, twin)

    def c_come(q, w):
        return remote(gs.at[tgt_at(z_off(-q), y if w == 0 else 1 - y, 1 - c)], cs, 2 * q + w, twin)

    def x_go(r):
        return remote(gt.at[s], xs, r - 1, (2 * x_off(r) + h, t))

    def x_come(r):
        return remote(gt.at[2 * x_off(-r) + h], xs, r - 1, partner)

    p_go = remote(gt.at[s], ps, 0, partner)
    p_come = remote(gt.at[2 * x + 1 - h], ps, 0, partner)

    def f_go(r):
        return remote(gt.at[2 * x + 1 - h], fs, r - 1, (2 * x_off(r) + h, t))

    def f_come(r):
        return remote(gt.at[2 * x_off(-r) + 1 - h], fs, r - 1, partner)

    near = sorted(range(1, nz), key=lambda r: min(r, nz - r))
    for r in reversed(near):
        z_go(r).start()
    p_go.start()
    y_go(0).start()
    for r in range(1, nx):
        x_go(r).start()
    c_go(0, 0).start()

    for f in fetches[2:]:
        f.wait()
    make_w1(c1, flat1, w1)

    events = []
    for n, r in enumerate(near):
        d = min(r, nz - r)
        events.append((0.9 + 0.75 * d, "z", r))
        events.append((0.9 + 0.75 * d + 1.7, "y", r))
    events += [(1.7, "y", 0), (2.75, "p", 0), (2.5, "w", 0), (3.6, "w", 1), (4.0, "w", 2)]
    for _, kind, q in sorted(events):
        if kind == "z":
            z_come(q).wait_recv()
            y_go(q).start()
            c_go(q, 0).start()
        elif kind == "y":
            y_come(q).wait_recv()
            c_go(q, 1).start()
        elif kind == "p":
            p_come.wait_recv()
            for r in range(1, nx):
                f_go(r).start()
        elif q == 0:
            make_w3(c3, flat3, w3)
        elif q == 1:
            make_w2(c2, w2)
        else:
            bias[0] = column(bs[0])
            bias[1] = column(bs[1])
            bias[2] = jnp.full((16, 128), b3_ref[0, 0], F32)

    for r in range(1, nx):
        x_come(r).wait_recv()
    for r in range(1, nx):
        f_come(r).wait_recv()
    sq = None
    for n in range(ns):
        v = gt[n].astype(F32)
        sq = v * v if sq is None else sq + v * v
    inv_t = inverse_root(jnp.sum(sq, axis=1, keepdims=True) + EPS)

    for q in range(nz):
        for w in range(2):
            c_come(q, w).wait_recv()
    sq = None
    for n in range(nt):
        v = gs[n].astype(F32)
        v = v * v
        for q in range(ch_s // 8):
            p = v[8 * q:8 * q + 8]
            sq = p if sq is None else sq + p
    inv_s = inverse_root(jnp.sum(sq, axis=0, keepdims=True) + EPS)

    per = ch_t // ch_s
    acc = jnp.zeros((128, 128), F32)
    for n in range(ns):
        left = jnp.concatenate([gs[n * per + q] for q in range(per)], 0)
        left = (left.astype(F32) * inv_s).astype(BF)
        right = (gt[n].astype(F32) * inv_t).astype(BF)
        acc = acc + jnp.dot(right, left, preferred_element_type=F32)
    v = acc.T
    block = iota((8, 128), 1) // 32
    for i in range(4):
        for k in range(4):
            u = None
            for hi in range(4):
                w = v[32 * i + 8 * hi:32 * i + 8 * hi + 8]
                w = pltpu.roll(w, (32 * (hi - k)) % 128, 1) if hi != k else w
                u = w if u is None else jnp.where(block == hi, w, u)
            u = u.astype(BF)
            own[i, k] = u
            vol[3 + i, 3 + k] = u

    def halo(n, ds, dt):
        i0, ni, i1 = halo_span(ds)
        k0, nk, k1 = halo_span(dt)
        return pltpu.make_async_remote_copy(
            src_ref=own.at[pl.ds(i0, ni), pl.ds(k0, nk)], dst_ref=vol.at[pl.ds(i1, ni), pl.ds(k1, nk)],
            send_sem=h_send.at[n], recv_sem=h_recv.at[n], device_id=(s + ds, t + dt), device_id_type=MESH)

    for n, (ds, dt) in enumerate(SIDES):
        @pl.when(there(ds, dt))
        def _():
            halo(n, ds, dt).start()

    for r in near:
        z_go(r).wait_send()
    for q in range(nz):
        y_go(q).wait_send()
        for w in range(2):
            c_go(q, w).wait_send()
    p_go.wait_send()
    for r in range(1, nx):
        x_go(r).wait_send()
        f_go(r).wait_send()

    for n, (ds, dt) in enumerate(SIDES):
        @pl.when(there(-ds, -dt))
        def _():
            halo(n, ds, dt).wait_recv()

    for n, (ds, dt) in enumerate(SIDES):
        @pl.when(there(ds, dt))
        def _():
            halo(n, ds, dt).wait_send()


def rolled(x, by):
    return pltpu.roll(x, by % 128, 1)


def conv_kernel(ns, nt, u_ref, w1_ref, w2_ref, w3_ref, bias_ref, o_ref, z, act1, act2, fin):
    s, t = lax.axis_index("src"), lax.axis_index("tgt")
    lane = lax.broadcasted_iota(jnp.int32, (8, 128), 1)
    row = lax.broadcasted_iota(jnp.int32, (8, 128), 0)
    lane16 = lax.broadcasted_iota(jnp.int32, (16, 128), 1)
    first8, last8 = lane % 32 == 0, lane % 32 == 31
    first, last = lane16 % 32 == 0, lane16 % 32 == 31
    dot = functools.partial(jnp.dot, preferred_element_type=F32)

    @pl.loop(0, 10)
    def _(i):
        for k in range(10):
            u = u_ref[i, k].astype(F32)
            before = jnp.where(lane >= 32, rolled(u, 32), 0.0)
            after = jnp.where(lane < 96, rolled(u, -32), 0.0)
            both = jnp.where(row >= 4, before, after)
            for g in range(3):
                if g == 0:
                    p, q = (jnp.where(first8, 0.0, rolled(v, 1)) for v in (u, both))
                elif g == 1:
                    p, q = u, both
                else:
                    p, q = (jnp.where(last8, 0.0, rolled(v, -1)) for v in (u, both))
                z[i, k, pl.ds(16 * g, 16)] = jnp.concatenate([p, q], 0).astype(BF)

    w1 = w1_ref[...]
    b1 = bias_ref[0]

    def put(act, i, k, j, v):
        act[i, k, 1 + j] = v.astype(BF)
        if j == 7:
            act[i, k, 0] = jnp.where(lane16 >= 32, rolled(v, 32), 0.0).astype(BF)
        if j == 0:
            act[i, k, 9] = jnp.where(lane16 < 96, rolled(v, -32), 0.0).astype(BF)

    def kept(i, k, off):
        gi, gk = 4 * s - off + i, 4 * t - off + k
        ok = (gi >= 0) & (gi < 4 * ns) & (gk >= 0) & (gk < 4 * nt)
        return jnp.where(ok, 1.0, 0.0)

    if 3 >= 1:
        @pl.loop(0, 8)
        def _(i):
            for kk in range(4):
                cols = []
                for m in range(2):
                    cols.append(jnp.concatenate(
                        [z[i + a, 2 * kk + m + e] for a in range(3) for e in range(3)], 0))
                y = dot(w1, jnp.concatenate(cols, 1))
                for m in range(2):
                    k = 2 * kk + m
                    keep = kept(i, k, 2)
                    for j in range(8):
                        v = jnp.maximum(y[16 * j:16 * j + 16, 128 * m:128 * m + 128] + b1, 0.0) * keep
                        put(act1, i, k, j, v)

    b2 = bias_ref[1]
    if 3 >= 2:
        @pl.loop(0, 3)
        def _(ii):
            for kk in range(3):
                for p in range(4):
                    cols = []
                    for m in range(2):
                        cols.append(jnp.concatenate(
                            [act1[2 * ii + a, 2 * kk + e, 2 * p + m + b]
                             for a in range(4) for e in range(4) for b in range(3)], 0))
                    y = dot(w2_ref[...], jnp.concatenate(cols, 1))
                    for di in range(2):
                        for dk in range(2):
                            i, k = 2 * ii + di, 2 * kk + dk
                            keep = kept(i, k, 1)
                            r = 48 * (2 * di + dk)
                            for m in range(2):
                                h = slice(128 * m, 128 * m + 128)
                                v = (y[r + 16:r + 32, h] + jnp.where(first, 0.0, rolled(y[r:r + 16, h], 1))
                                     + jnp.where(last, 0.0, rolled(y[r + 32:r + 48, h], -1)) + b2)
                                put(act2, i, k, 2 * p + m, jnp.maximum(v, 0.0) * keep)

    w3 = w3_ref[...]
    b3 = bias_ref[2, pl.ds(0, 8)]
    if 3 >= 3:
        for ii in range(2):
            for kk in range(2):
                per_col = []
                for q in range(5):
                    y = dot(w3, jnp.concatenate([jnp.concatenate(
                        [act2[2 * ii + a, 2 * kk + e, 2 * q + m] for a in range(4) for e in range(4)], 0)
                        for m in range(2)], 1))
                    per_col += [y[:, 0:128], y[:, 128:256]]
                buf = fin.at[2 * ii + kk]
                for j in range(8):
                    v = per_col[j][0:16] + per_col[j + 1][16:32] + per_col[j + 2][32:48]
                    left = pltpu.roll(jnp.where(first8, 0.0, rolled(v[0:8], 1)), 4, 0)
                    v = v[0:8] + left + jnp.where(last8, 0.0, rolled(v[8:16], -1)) + b3
                    buf[pl.ds(8 * j, 8)] = jnp.maximum(v, 0.0)
                for di in range(2):
                    for dk in range(2):
                        v = buf[pl.ds(2 * di + dk, 8, stride=8), :]
                        o_ref[2 * ii + di, 2 * kk + dk] = jnp.concatenate(
                            [v[:, 32 * q:32 * q + 32] for q in range(4)], 0).astype(BF)


def whole_kernel(ns, nt, *refs):
    given, (out, vol, w1, w2, w3, bias, z, act1, act2, fin), rest = refs[:8], refs[8:18], refs[18:]
    volume_kernel(ns, nt, *given, vol, w1, w2, w3, bias, *rest)
    conv_kernel(ns, nt, vol, w1, w2, w3, bias, out, z, act1, act2, fin)


def whole_call(ns, nt, *given):
    src, tgt = given[:2]
    hbm = pl.BlockSpec(memory_space=pl.ANY)
    vmem, dma = pltpu.VMEM, pltpu.SemaphoreType.DMA
    pairs = [nt // 4 - 1, nt // 4, nt // 2, ns // 2 - 1, 1, ns // 2 - 1, 8]
    return pl.pallas_call(
        functools.partial(whole_kernel, ns, nt),
        out_shape=jax.ShapeDtypeStruct((4, 4, 32, 32), BF),
        in_specs=[hbm] * 7 + [pl.BlockSpec(memory_space=pltpu.SMEM)],
        out_specs=pl.BlockSpec(memory_space=pltpu.VMEM),
        scratch_shapes=[
            vmem((10, 10, 8, 128), BF), vmem((128, 432), BF), vmem((192, 768), BF), vmem((48, 256), BF),
            vmem((3, 16, 128), F32),
            vmem((10, 10, 48, 128), BF), vmem((8, 8, 10, 16, 128), BF), vmem((6, 6, 10, 16, 128), BF),
            vmem((4, 64, 128), F32),
            vmem(src.shape, BF), vmem((nt, src.shape[-1], 128), BF), vmem((ns, 128, tgt.shape[-1]), BF),
            vmem((4, 4, 8, 128), BF),
            vmem((27, 3, 16), BF), vmem((81, 16, 16), BF), vmem((27, 3, 16), BF), vmem((2, 1, 16), F32),
            vmem((128, 128), F32), vmem((128, 128), F32),
            dma((7,)),
        ] + [dma((max(n, 1),)) for n in pairs for _ in range(2)],
        compiler_params=pltpu.CompilerParams(
            collective_id=0, has_side_effects=True, vmem_limit_bytes=65000000),
    )(*given)


def solution(mesh):
    ns, nt = mesh.shape["src"], mesh.shape["tgt"]

    def local(source, target, conv_one, bias_one, conv_two, bias_two, conv_three, bias_three):
        out = whole_call(
            ns, nt, source.reshape(128, -1), target.reshape(128, -1),
            conv_one.reshape(27, 3, 16), bias_one.reshape(1, 16), conv_two.reshape(81, 16, 16),
            bias_two.reshape(1, 16), conv_three.reshape(27, 3, 16), bias_three.reshape(1, 1))
        return out[None]

    return jax.shard_map(
        local,
        mesh=mesh,
        in_specs=(P(None, "src", None, "tgt"), P(None, "tgt", None, "src")) + (P(),) * 6,
        out_specs=P(None, "src", "tgt", None, None),
        check_vma=False,
    )
```

```python
import functools

import jax
import jax.numpy as jnp
from jax import lax
from jax.experimental import pallas as pl
from jax.experimental.pallas import tpu as pltpu
from jax.sharding import PartitionSpec as P

F32, BF = jnp.float32, jnp.bfloat16

MESH = pl.DeviceIdType.MESH
EPS = 1e-6
SIDES = [(ds, dt) for ds in (-1, 0, 1) for dt in (-1, 0, 1) if ds or dt]
NT = (((1,), (1,)), ((), ()))


def halo_span(d):
    if d == 0:
        return 0, 4, 3
    return (1, 3, 0) if d > 0 else (0, 3, 7)


def iota(shape, dim):
    return lax.broadcasted_iota(jnp.int32, shape, dim)


def hot(mask):
    return jnp.where(mask, 1.0, 0.0).astype(BF)


def make_w1(c1, flat, w1):
    flat[...] = jnp.zeros_like(flat)
    for n in range(27):
        flat[pl.ds(3 * n, 3), pl.ds(0, 16)] = c1[n].astype(F32)
    xt = flat[...].T[0:16, 0:96].astype(BF)
    n = iota((1, 432), 1)
    a, e, g, at = n // 144, (n // 48) % 3, (n // 16) % 3, n % 16
    at = jnp.where(at == 15, -1, jnp.where(at <= 8, at, 100))
    base = a * 27 + e * 3 + g
    r = iota((96, 432), 0)
    for j in range(8):
        b = at - j + 1
        key = jnp.where((b >= 0) & (b < 3), base + 9 * b, -1)
        w1[pl.ds(16 * j, 16)] = jnp.dot(xt, hot(r == key), preferred_element_type=F32).astype(BF)


def make_w2(c2, w2):
    eye = hot(iota((16, 16), 0) == iota((16, 16), 1))
    none = jnp.zeros((16, 16), BF)
    for i in range(2):
        for k in range(2):
            for g in range(3):
                pieces = []
                for up in range(4):
                    for across in range(4):
                        for b in range(3):
                            a, e = up - i, across - k
                            inside = 0 <= a < 3 and 0 <= e < 3
                            pieces.append(c2[((a * 3 + b) * 3 + e) * 3 + g] if inside else none)
                w2[pl.ds(((2 * i + k) * 3 + g) * 16, 16)] = lax.dot_general(
                    eye, jnp.concatenate(pieces, 0), NT, preferred_element_type=F32).astype(BF)


def make_w3(c3, flat, w3):
    flat[...] = jnp.zeros_like(flat)
    for n in range(27):
        flat[pl.ds(3 * n, 3), pl.ds(0, 16)] = c3[n].astype(F32)
    y = flat[pl.ds(0, 96), pl.ds(0, 16)].astype(BF)
    wide = jnp.dot(y, hot(iota((16, 256), 1) % 16 == iota((16, 256), 0)), preferred_element_type=F32).astype(BF)
    m = iota((48, 1), 0)
    b, slot = m // 16, (m % 16) // 4
    g = jnp.where(slot == 0, 1, jnp.where(slot == 1, 0, 2))
    r = iota((48, 96), 1)
    mm, nn = iota((48, 256), 0), iota((48, 256), 1)
    up, across = nn // 64 - (mm // 2) % 2, (nn // 16) % 4 - mm % 2
    total = jnp.zeros((48, 256), F32)
    for a in range(3):
        for e in range(3):
            key = jnp.where(slot < 3, a * 27 + b * 9 + e * 3 + g, -1)
            part = jnp.dot(hot(r == key), wide, preferred_element_type=F32)
            total = total + jnp.where((up == a) & (across == e), part, 0.0)
    w3[...] = total.astype(BF)


def inverse_root(v):
    r = lax.rsqrt(v)
    return r * (1.5 - 0.5 * v * r * r)


def column(row):
    square = jnp.where(iota((16, 16), 0) == iota((16, 16), 1), jnp.broadcast_to(row, (16, 16)), 0.0)
    return jnp.broadcast_to(jnp.sum(square, axis=1, keepdims=True), (16, 128))


def volume_kernel(ns, nt, meanwhile, src_hbm, tgt_hbm, c1_hbm, b1_hbm, c2_hbm, b2_hbm, c3_hbm, b3_ref,
                  vol, w1, w2, w3, bias,
                  src, gs, gt, own, c1, c2, c3, bs, flat1, flat3, load,
                  z_send, z_recv, y_send, y_recv, c_send, c_recv, x_send, x_recv, p_send, p_recv,
                  f_send, f_recv, h_send, h_recv):
    s, t = lax.axis_index("src"), lax.axis_index("tgt")
    nz, nx = nt // 4, ns // 2
    z, y, c = t // 4, (t // 2) % 2, t % 2
    x, h = s // 2, s % 2
    ch_s, ch_t = src.shape[-1], gt.shape[-1]

    fetches = [pltpu.make_async_copy(a, b, load.at[n]) for n, (a, b) in enumerate(
        [(src_hbm, src), (tgt_hbm, gt.at[s]), (c1_hbm, c1), (c2_hbm, c2), (c3_hbm, c3),
         (b1_hbm, bs.at[0]), (b2_hbm, bs.at[1])])]
    for f in fetches:
        f.start()

    vol[...] = jnp.zeros_like(vol)

    def tgt_at(zz, yy, cc):
        return 4 * zz + 2 * yy + cc

    def z_off(r):
        return lax.rem(z + r + nz, nz)

    def x_off(r):
        return lax.rem(x + r + nx, nx)

    def there(ds, dt):
        return (s + ds >= 0) & (s + ds < ns) & (t + dt >= 0) & (t + dt < nt)

    barrier = pltpu.get_barrier_semaphore()
    peers = [(s, tgt_at(z_off(r), y, c)) for r in range(1, nz)]
    peers += [(s, tgt_at(z, 1 - y, c)), (s, tgt_at(z, 1 - y, 1 - c)), (s, tgt_at(z, y, 1 - c))]
    peers += [(2 * x_off(r) + h, t) for r in range(1, nx)] + [(2 * x + 1 - h, t)]
    count = len(peers)
    for p in peers:
        pl.semaphore_signal(barrier, inc=1, device_id=p, device_id_type=MESH)
    for ds, dt in SIDES:
        count = count + jnp.where(there(ds, dt), 1, 0)

        @pl.when(there(ds, dt))
        def _():
            pl.semaphore_signal(barrier, inc=1, device_id=(s + ds, t + dt), device_id_type=MESH)

    fetches[0].wait()
    eye = hot(iota((ch_s, ch_s), 0) == iota((ch_s, ch_s), 1))
    gs[t] = lax.dot_general(eye, src[...], NT, preferred_element_type=F32).astype(BF)
    fetches[1].wait()
    pl.semaphore_wait(barrier, count)

    def remote(ref, sems, n, to):
        return pltpu.make_async_remote_copy(
            src_ref=ref, dst_ref=ref, send_sem=sems[0].at[n], recv_sem=sems[1].at[n],
            device_id=to, device_id_type=MESH)

    zs, ys, cs, xs, ps, fs = ((z_send, z_recv), (y_send, y_recv), (c_send, c_recv), (x_send, x_recv),
                              (p_send, p_recv), (f_send, f_recv))
    mate, twin, partner = (s, tgt_at(z, 1 - y, c)), (s, tgt_at(z, y, 1 - c)), (2 * x + 1 - h, t)
    across = (s, tgt_at(z, 1 - y, 1 - c))

    def z_go(r):
        return remote(gs.at[t], zs, r - 1, (s, tgt_at(z_off(r), y, c)))

    def z_come(r):
        return remote(gs.at[tgt_at(z_off(-r), y, c)], zs, r - 1, mate)

    def y_go(q):
        return remote(gs.at[tgt_at(z_off(-q), y, c)], ys, q, mate)

    def y_come(q):
        return remote(gs.at[tgt_at(z_off(-q), 1 - y, c)], ys, q, mate)

    def c_go(q, w):
        return remote(gs.at[tgt_at(z_off(-q), y, c)], cs, 2 * q + w, twin if w == 0 else across)

    def c_come(q, w):
        return remote(gs.at[tgt_at(z_off(-q), y if w == 0 else 1 - y, 1 - c)], cs, 2 * q + w, twin)

    def x_go(r):
        return remote(gt.at[s], xs, r - 1, (2 * x_off(r) + h, t))

    def x_come(r):
        return remote(gt.at[2 * x_off(-r) + h], xs, r - 1, partner)

    p_go = remote(gt.at[s], ps, 0, partner)
    p_come = remote(gt.at[2 * x + 1 - h], ps, 0, partner)

    def f_go(r):
        return remote(gt.at[2 * x + 1 - h], fs, r - 1, (2 * x_off(r) + h, t))

    def f_come(r):
        return remote(gt.at[2 * x_off(-r) + 1 - h], fs, r - 1, partner)

    near = sorted(range(1, nz), key=lambda r: min(r, nz - r))
    for r in reversed(near):
        z_go(r).start()
    p_go.start()
    y_go(0).start()
    c_go(0, 1).start()
    for r in range(1, nx):
        x_go(r).start()
    c_go(0, 0).start()

    for f in fetches[2:]:
        f.wait()
    make_w1(c1, flat1, w1)

    events = []
    for n, r in enumerate(near):
        d = min(r, nz - r)
        events.append((0.9 + 0.75 * d, "z", r))
    events += [(2.75, "p", 0), (2.5, "w", 0), (3.6, "w", 1), (4.0, "w", 2)]
    for _, kind, q in sorted(events):
        if kind == "z":
            z_come(q).wait_recv()
            y_go(q).start()
            c_go(q, 1).start()
            c_go(q, 0).start()
        elif kind == "p":
            p_come.wait_recv()
            for r in range(1, nx):
                f_go(r).start()
        elif q == 0:
            make_w3(c3, flat3, w3)
        elif q == 1:
            make_w2(c2, w2)
        else:
            bias[0] = column(bs[0])
            bias[1] = column(bs[1])
            bias[2] = jnp.full((16, 128), b3_ref[0, 0], F32)

    for r in range(1, nx):
        x_come(r).wait_recv()
    for r in range(1, nx):
        f_come(r).wait_recv()
    sq = None
    for n in range(ns):
        v = gt[n].astype(F32)
        sq = v * v if sq is None else sq + v * v
    inv_t = inverse_root(jnp.sum(sq, axis=1, keepdims=True) + EPS)

    for q in range(nz):
        y_come(q).wait_recv()
        for w in range(2):
            c_come(q, w).wait_recv()
    sq = None
    for n in range(nt):
        v = gs[n].astype(F32)
        v = v * v
        for q in range(ch_s // 8):
            p = v[8 * q:8 * q + 8]
            sq = p if sq is None else sq + p
    inv_s = inverse_root(jnp.sum(sq, axis=0, keepdims=True) + EPS)

    per = ch_t // ch_s
    acc = jnp.zeros((128, 128), F32)
    for n in range(ns):
        left = jnp.concatenate([gs[n * per + q] for q in range(per)], 0)
        left = (left.astype(F32) * inv_s).astype(BF)
        right = (gt[n].astype(F32) * inv_t).astype(BF)
        acc = acc + jnp.dot(right, left, preferred_element_type=F32)
    v = acc.T
    block = iota((8, 128), 1) // 32
    for i in range(4):
        for k in range(4):
            u = None
            for hi in range(4):
                w = v[32 * i + 8 * hi:32 * i + 8 * hi + 8]
                w = pltpu.roll(w, (32 * (hi - k)) % 128, 1) if hi != k else w
                u = w if u is None else jnp.where(block == hi, w, u)
            u = u.astype(BF)
            own[i, k] = u
            vol[3 + i, 3 + k] = u

    def halo(n, ds, dt):
        i0, ni, i1 = halo_span(ds)
        k0, nk, k1 = halo_span(dt)
        return pltpu.make_async_remote_copy(
            src_ref=own.at[pl.ds(i0, ni), pl.ds(k0, nk)], dst_ref=vol.at[pl.ds(i1, ni), pl.ds(k1, nk)],
            send_sem=h_send.at[n], recv_sem=h_recv.at[n], device_id=(s + ds, t + dt), device_id_type=MESH)

    for n, (ds, dt) in enumerate(SIDES):
        @pl.when(there(ds, dt))
        def _():
            halo(n, ds, dt).start()

    def arrived(wanted):
        for n, (ds, dt) in enumerate(SIDES):
            if wanted(ds):
                @pl.when(there(-ds, -dt))
                def _():
                    halo(n, ds, dt).wait_recv()

    arrived(lambda ds: ds == 0)
    meanwhile()
    arrived(lambda ds: ds != 0)

    for r in near:
        z_go(r).wait_send()
    for q in range(nz):
        y_go(q).wait_send()
        for w in range(2):
            c_go(q, w).wait_send()
    p_go.wait_send()
    for r in range(1, nx):
        x_go(r).wait_send()
        f_go(r).wait_send()

    for n, (ds, dt) in enumerate(SIDES):
        @pl.when(there(ds, dt))
        def _():
            halo(n, ds, dt).wait_send()


def rolled(x, by):
    return pltpu.roll(x, by % 128, 1)


def conv_stages(ns, nt, u_ref, w1_ref, w2_ref, w3_ref, bias_ref, o_ref, z, act1, act2, fin):
    s, t = lax.axis_index("src"), lax.axis_index("tgt")
    lane = lax.broadcasted_iota(jnp.int32, (8, 128), 1)
    row = lax.broadcasted_iota(jnp.int32, (8, 128), 0)
    lane16 = lax.broadcasted_iota(jnp.int32, (16, 128), 1)
    first8, last8 = lane % 32 == 0, lane % 32 == 31
    first, last = lane16 % 32 == 0, lane16 % 32 == 31
    dot = functools.partial(jnp.dot, preferred_element_type=F32)

    def pieces(lo, hi):
        @pl.loop(lo, hi)
        def _(i):
            for k in range(10):
                u = u_ref[i, k].astype(F32)
                before = jnp.where(lane >= 32, rolled(u, 32), 0.0)
                after = jnp.where(lane < 96, rolled(u, -32), 0.0)
                both = jnp.where(row >= 4, before, after)
                for g in range(3):
                    if g == 0:
                        p, q = (jnp.where(first8, 0.0, rolled(v, 1)) for v in (u, both))
                    elif g == 1:
                        p, q = u, both
                    else:
                        p, q = (jnp.where(last8, 0.0, rolled(v, -1)) for v in (u, both))
                    z[i, k, pl.ds(16 * g, 16)] = jnp.concatenate([p, q], 0).astype(BF)


    def put(act, i, k, j, v):
        act[i, k, 1 + j] = v.astype(BF)
        if j == 7:
            act[i, k, 0] = jnp.where(lane16 >= 32, rolled(v, 32), 0.0).astype(BF)
        if j == 0:
            act[i, k, 9] = jnp.where(lane16 < 96, rolled(v, -32), 0.0).astype(BF)

    def kept(i, k, off):
        gi, gk = 4 * s - off + i, 4 * t - off + k
        ok = (gi >= 0) & (gi < 4 * ns) & (gk >= 0) & (gk < 4 * nt)
        return jnp.where(ok, 1.0, 0.0)

    def layer_one(lo, hi):
        w1, b1 = w1_ref[...], bias_ref[0]

        @pl.loop(lo, hi)
        def _(i):
            for kk in range(4):
                cols = []
                for m in range(2):
                    cols.append(jnp.concatenate(
                        [z[i + a, 2 * kk + m + e] for a in range(3) for e in range(3)], 0))
                y = dot(w1, jnp.concatenate(cols, 1))
                for m in range(2):
                    k = 2 * kk + m
                    keep = kept(i, k, 2)
                    for j in range(8):
                        v = jnp.maximum(y[16 * j:16 * j + 16, 128 * m:128 * m + 128] + b1, 0.0) * keep
                        put(act1, i, k, j, v)

    def rest():
        b2 = bias_ref[1]
        @pl.loop(0, 3)
        def _(ii):
            for kk in range(3):
                for p in range(4):
                    cols = []
                    for m in range(2):
                        cols.append(jnp.concatenate(
                            [act1[2 * ii + a, 2 * kk + e, 2 * p + m + b]
                             for a in range(4) for e in range(4) for b in range(3)], 0))
                    y = dot(w2_ref[...], jnp.concatenate(cols, 1))
                    for di in range(2):
                        for dk in range(2):
                            i, k = 2 * ii + di, 2 * kk + dk
                            keep = kept(i, k, 1)
                            r = 48 * (2 * di + dk)
                            for m in range(2):
                                h = slice(128 * m, 128 * m + 128)
                                v = (y[r + 16:r + 32, h] + jnp.where(first, 0.0, rolled(y[r:r + 16, h], 1))
                                     + jnp.where(last, 0.0, rolled(y[r + 32:r + 48, h], -1)) + b2)
                                put(act2, i, k, 2 * p + m, jnp.maximum(v, 0.0) * keep)

        w3 = w3_ref[...]
        b3 = bias_ref[2, pl.ds(0, 8)]
        for ii in range(2):
            for kk in range(2):
                per_col = []
                for q in range(5):
                    y = dot(w3, jnp.concatenate([jnp.concatenate(
                        [act2[2 * ii + a, 2 * kk + e, 2 * q + m] for a in range(4) for e in range(4)], 0)
                        for m in range(2)], 1))
                    per_col += [y[:, 0:128], y[:, 128:256]]
                buf = fin.at[2 * ii + kk]
                for j in range(8):
                    v = per_col[j][0:16] + per_col[j + 1][16:32] + per_col[j + 2][32:48]
                    left = pltpu.roll(jnp.where(first8, 0.0, rolled(v[0:8], 1)), 4, 0)
                    v = v[0:8] + left + jnp.where(last8, 0.0, rolled(v[8:16], -1)) + b3
                    buf[pl.ds(8 * j, 8)] = jnp.maximum(v, 0.0)
                for di in range(2):
                    for dk in range(2):
                        v = buf[pl.ds(2 * di + dk, 8, stride=8), :]
                        o_ref[2 * ii + di, 2 * kk + dk] = jnp.concatenate(
                            [v[:, 32 * q:32 * q + 32] for q in range(4)], 0).astype(BF)

    return pieces, layer_one, rest


def whole_kernel(ns, nt, *refs):
    given, (out, vol, w1, w2, w3, bias, z, act1, act2, fin), rest = refs[:8], refs[8:18], refs[18:]
    pieces, layer_one, others = conv_stages(ns, nt, vol, w1, w2, w3, bias, out, z, act1, act2, fin)

    def meanwhile():
        pieces(3, 7)
        layer_one(3, 5)

    volume_kernel(ns, nt, meanwhile, *given, vol, w1, w2, w3, bias, *rest)
    pieces(0, 3)
    pieces(7, 10)
    layer_one(0, 3)
    layer_one(5, 8)
    others()


def whole_call(ns, nt, *given):
    src, tgt = given[:2]
    hbm = pl.BlockSpec(memory_space=pl.ANY)
    vmem, dma = pltpu.VMEM, pltpu.SemaphoreType.DMA
    pairs = [nt // 4 - 1, nt // 4, nt // 2, ns // 2 - 1, 1, ns // 2 - 1, 8]
    return pl.pallas_call(
        functools.partial(whole_kernel, ns, nt),
        out_shape=pltpu.VMEM((4, 4, 32, 32), BF),
        in_specs=[hbm] * 7 + [pl.BlockSpec(memory_space=pltpu.SMEM)],
        out_specs=pl.BlockSpec(memory_space=pltpu.VMEM),
        scratch_shapes=[
            vmem((10, 10, 8, 128), BF), vmem((128, 432), BF), vmem((192, 768), BF), vmem((48, 256), BF),
            vmem((3, 16, 128), F32),
            vmem((10, 10, 48, 128), BF), vmem((8, 8, 10, 16, 128), BF), vmem((6, 6, 10, 16, 128), BF),
            vmem((4, 64, 128), F32),
            vmem(src.shape, BF), vmem((nt, src.shape[-1], 128), BF), vmem((ns, 128, tgt.shape[-1]), BF),
            vmem((4, 4, 8, 128), BF),
            vmem((27, 3, 16), BF), vmem((81, 16, 16), BF), vmem((27, 3, 16), BF), vmem((2, 1, 16), F32),
            vmem((128, 128), F32), vmem((128, 128), F32),
            dma((7,)),
        ] + [dma((max(n, 1),)) for n in pairs for _ in range(2)],
        compiler_params=pltpu.CompilerParams(
            collective_id=0, has_side_effects=True, vmem_limit_bytes=65000000),
    )(*given)


def solution(mesh):
    ns, nt = mesh.shape["src"], mesh.shape["tgt"]

    def local(source, target, conv_one, bias_one, conv_two, bias_two, conv_three, bias_three):
        out = whole_call(
            ns, nt, source.reshape(128, -1), target.reshape(128, -1),
            conv_one.reshape(27, 3, 16), bias_one.reshape(1, 16), conv_two.reshape(81, 16, 16),
            bias_two.reshape(1, 16), conv_three.reshape(27, 3, 16), bias_three.reshape(1, 1))
        return out[None]

    return jax.shard_map(
        local,
        mesh=mesh,
        in_specs=(P(None, "src", None, "tgt"), P(None, "tgt", None, "src")) + (P(),) * 6,
        out_specs=P(None, "src", "tgt", None, None),
        check_vma=False,
    )
```

```python
import functools

import jax
import jax.numpy as jnp
from jax import lax
from jax.experimental import pallas as pl
from jax.experimental.pallas import tpu as pltpu
from jax.sharding import PartitionSpec as P

F32, BF = jnp.float32, jnp.bfloat16

MESH = pl.DeviceIdType.MESH
EPS = 1e-6
SIDES = [(ds, dt) for ds in (-1, 0, 1) for dt in (-1, 0, 1) if ds or dt]
NT = (((1,), (1,)), ((), ()))


def halo_span(d):
    if d == 0:
        return 0, 4, 3
    return (1, 3, 0) if d > 0 else (0, 3, 7)


def iota(shape, dim):
    return lax.broadcasted_iota(jnp.int32, shape, dim)


def hot(mask):
    return jnp.where(mask, 1.0, 0.0).astype(BF)


def make_w1(c1, flat, w1):
    flat[...] = jnp.zeros_like(flat)
    for n in range(27):
        flat[pl.ds(3 * n, 3), pl.ds(0, 16)] = c1[n].astype(F32)
    xt = flat[...].T[0:16, 0:96].astype(BF)
    n = iota((1, 192), 1)
    a, across, half, at = n // 64, (n // 16) % 4, (n % 16) // 8, n % 8
    r = iota((96, 192), 0)
    for q in range(3):
        d = (at - (3 * q - 1) + 8) % 8
        from_ = jnp.where(d <= 4, d, jnp.where(half == 0, d - 5, d - 2))
        g = jnp.where(d <= 4, 2 * half, 1)
        for j in range(3 if q < 2 else 2):
            b = from_ - j
            for k in range(2):
                e = across - k
                inside = (from_ <= 4) & (b >= 0) & (b < 3) & (e >= 0) & (e < 3)
                key = jnp.where(inside, a * 27 + b * 9 + e * 3 + g, -1)
                w1[pl.ds(96 * q + 32 * j + 16 * k, 16)] = jnp.dot(
                    xt, hot(r == key), preferred_element_type=F32).astype(BF)


def make_w2(c2, w2):
    eye = hot(iota((16, 16), 0) == iota((16, 16), 1))
    none = jnp.zeros((16, 16), BF)
    for i in range(2):
        for k in range(2):
            for g in range(3):
                pieces = []
                for up in range(4):
                    for across in range(4):
                        for b in range(3):
                            a, e = up - i, across - k
                            inside = 0 <= a < 3 and 0 <= e < 3
                            pieces.append(c2[((a * 3 + b) * 3 + e) * 3 + g] if inside else none)
                w2[pl.ds(((2 * i + k) * 3 + g) * 16, 16)] = lax.dot_general(
                    eye, jnp.concatenate(pieces, 0), NT, preferred_element_type=F32).astype(BF)


def make_w3(c3, flat, w3):
    flat[...] = jnp.zeros_like(flat)
    for n in range(27):
        flat[pl.ds(3 * n, 3), pl.ds(0, 16)] = c3[n].astype(F32)
    y = flat[pl.ds(0, 96), pl.ds(0, 16)].astype(BF)
    wide = jnp.dot(y, hot(iota((16, 256), 1) % 16 == iota((16, 256), 0)), preferred_element_type=F32).astype(BF)
    m = iota((48, 1), 0)
    b, slot = m // 16, (m % 16) // 4
    g = jnp.where(slot == 0, 1, jnp.where(slot == 1, 0, 2))
    r = iota((48, 96), 1)
    mm, nn = iota((48, 256), 0), iota((48, 256), 1)
    up, across = nn // 64 - (mm // 2) % 2, (nn // 16) % 4 - mm % 2
    total = jnp.zeros((48, 256), F32)
    for a in range(3):
        for e in range(3):
            key = jnp.where(slot < 3, a * 27 + b * 9 + e * 3 + g, -1)
            part = jnp.dot(hot(r == key), wide, preferred_element_type=F32)
            total = total + jnp.where((up == a) & (across == e), part, 0.0)
    w3[...] = total.astype(BF)


def inverse_root(v):
    r = lax.rsqrt(v)
    return r * (1.5 - 0.5 * v * r * r)


def column(row):
    square = jnp.where(iota((16, 16), 0) == iota((16, 16), 1), jnp.broadcast_to(row, (16, 16)), 0.0)
    return jnp.broadcast_to(jnp.sum(square, axis=1, keepdims=True), (16, 128))


def volume_kernel(ns, nt, meanwhile, src_hbm, tgt_hbm, c1_hbm, b1_hbm, c2_hbm, b2_hbm, c3_hbm, b3_ref,
                  vol, w1, w2, w3, bias,
                  src, gs, gt, own, c1, c2, c3, bs, flat1, flat3, load,
                  z_send, z_recv, y_send, y_recv, c_send, c_recv, x_send, x_recv, p_send, p_recv,
                  f_send, f_recv, h_send, h_recv):
    s, t = lax.axis_index("src"), lax.axis_index("tgt")
    nz, nx = nt // 4, ns // 2
    z, y, c = t // 4, (t // 2) % 2, t % 2
    x, h = s // 2, s % 2
    ch_s, ch_t = src.shape[-1], gt.shape[-1]

    fetches = [pltpu.make_async_copy(a, b, load.at[n]) for n, (a, b) in enumerate(
        [(src_hbm, src), (tgt_hbm, gt.at[s]), (c1_hbm, c1), (c2_hbm, c2), (c3_hbm, c3),
         (b1_hbm, bs.at[0]), (b2_hbm, bs.at[1])])]
    for f in fetches:
        f.start()

    vol[...] = jnp.zeros_like(vol)

    def tgt_at(zz, yy, cc):
        return 4 * zz + 2 * yy + cc

    def z_off(r):
        return lax.rem(z + r + nz, nz)

    def x_off(r):
        return lax.rem(x + r + nx, nx)

    def there(ds, dt):
        return (s + ds >= 0) & (s + ds < ns) & (t + dt >= 0) & (t + dt < nt)

    barrier = pltpu.get_barrier_semaphore()
    peers = [(s, tgt_at(z_off(r), y, c)) for r in range(1, nz)]
    peers += [(s, tgt_at(z, 1 - y, c)), (s, tgt_at(z, 1 - y, 1 - c)), (s, tgt_at(z, y, 1 - c))]
    peers += [(2 * x_off(r) + h, t) for r in range(1, nx)] + [(2 * x + 1 - h, t)]
    count = len(peers)
    for p in peers:
        pl.semaphore_signal(barrier, inc=1, device_id=p, device_id_type=MESH)
    for ds, dt in SIDES:
        count = count + jnp.where(there(ds, dt), 1, 0)

        @pl.when(there(ds, dt))
        def _():
            pl.semaphore_signal(barrier, inc=1, device_id=(s + ds, t + dt), device_id_type=MESH)

    fetches[0].wait()
    eye = hot(iota((ch_s, ch_s), 0) == iota((ch_s, ch_s), 1))
    gs[t] = lax.dot_general(eye, src[...], NT, preferred_element_type=F32).astype(BF)
    fetches[1].wait()
    pl.semaphore_wait(barrier, count)

    def remote(ref, sems, n, to):
        return pltpu.make_async_remote_copy(
            src_ref=ref, dst_ref=ref, send_sem=sems[0].at[n], recv_sem=sems[1].at[n],
            device_id=to, device_id_type=MESH)

    zs, ys, cs, xs, ps, fs = ((z_send, z_recv), (y_send, y_recv), (c_send, c_recv), (x_send, x_recv),
                              (p_send, p_recv), (f_send, f_recv))
    mate, twin, partner = (s, tgt_at(z, 1 - y, c)), (s, tgt_at(z, y, 1 - c)), (2 * x + 1 - h, t)
    across = (s, tgt_at(z, 1 - y, 1 - c))

    def z_go(r):
        return remote(gs.at[t], zs, r - 1, (s, tgt_at(z_off(r), y, c)))

    def z_come(r):
        return remote(gs.at[tgt_at(z_off(-r), y, c)], zs, r - 1, mate)

    def y_go(q):
        return remote(gs.at[tgt_at(z_off(-q), y, c)], ys, q, mate)

    def y_come(q):
        return remote(gs.at[tgt_at(z_off(-q), 1 - y, c)], ys, q, mate)

    def c_go(q, w):
        return remote(gs.at[tgt_at(z_off(-q), y, c)], cs, 2 * q + w, twin if w == 0 else across)

    def c_come(q, w):
        return remote(gs.at[tgt_at(z_off(-q), y if w == 0 else 1 - y, 1 - c)], cs, 2 * q + w, twin)

    def half(ref, m):
        return ref.at[pl.ds(64 * m, 64)]

    def x_go(r):
        return remote(gt.at[s], xs, r - 1, (2 * x_off(r) + h, t))

    def x_come(r):
        return remote(gt.at[2 * x_off(-r) + h], xs, r - 1, partner)

    def p_go(m):
        return remote(half(gt.at[s], m), ps, m, partner)

    def p_come(m):
        return remote(half(gt.at[2 * x + 1 - h], m), ps, m, partner)

    def f_go(r, m):
        return remote(half(gt.at[2 * x + 1 - h], m), fs, 2 * r - 2 + m, (2 * x_off(r) + h, t))

    def f_come(r, m):
        return remote(half(gt.at[2 * x_off(-r) + 1 - h], m), fs, 2 * r - 2 + m, partner)

    far = sorted(range(1, nx), key=lambda r: -min(r, nx - r))

    near = sorted(range(1, nz), key=lambda r: min(r, nz - r))
    for r in reversed(near):
        z_go(r).start()
    p_go(0).start()
    p_go(1).start()
    y_go(0).start()
    c_go(0, 1).start()
    for r in range(1, nx):
        x_go(r).start()
    c_go(0, 0).start()

    for f in fetches[2:]:
        f.wait()
    make_w1(c1, flat1, w1)

    events = []
    for n, r in enumerate(near):
        d = min(r, nz - r)
        events.append((0.9 + 0.75 * d, "z", r))
    events += [(2.6, "p", 0), (2.8, "p", 1), (2.5, "w", 0), (3.6, "w", 1), (4.0, "w", 2)]
    for _, kind, q in sorted(events):
        if kind == "z":
            z_come(q).wait_recv()
            y_go(q).start()
            c_go(q, 1).start()
            c_go(q, 0).start()
        elif kind == "p":
            p_come(q).wait_recv()
            for r in far:
                f_go(r, q).start()
        elif q == 0:
            make_w3(c3, flat3, w3)
        elif q == 1:
            make_w2(c2, w2)
        else:
            bias[0] = column(bs[0])
            bias[1] = column(bs[1])
            bias[2] = jnp.full((16, 128), b3_ref[0, 0], F32)

    for r in range(1, nx):
        x_come(r).wait_recv()
    for r in range(1, nx):
        for m in range(2):
            f_come(r, m).wait_recv()
    sq = None
    for n in range(ns):
        v = gt[n].astype(F32)
        sq = v * v if sq is None else sq + v * v
    inv_t = inverse_root(jnp.sum(sq, axis=1, keepdims=True) + EPS)

    for q in range(nz):
        y_come(q).wait_recv()
        for w in range(2):
            c_come(q, w).wait_recv()
    sq = None
    for n in range(nt):
        v = gs[n].astype(F32)
        v = v * v
        for q in range(ch_s // 8):
            p = v[8 * q:8 * q + 8]
            sq = p if sq is None else sq + p
    inv_s = inverse_root(jnp.sum(sq, axis=0, keepdims=True) + EPS)

    per = ch_t // ch_s
    acc = jnp.zeros((128, 128), F32)
    for n in range(ns):
        left = jnp.concatenate([gs[n * per + q] for q in range(per)], 0)
        left = (left.astype(F32) * inv_s).astype(BF)
        right = (gt[n].astype(F32) * inv_t).astype(BF)
        acc = acc + jnp.dot(right, left, preferred_element_type=F32)
    v = acc.T
    block = iota((8, 128), 1) // 32
    for i in range(4):
        for k in range(4):
            u = None
            for hi in range(4):
                w = v[32 * i + 8 * hi:32 * i + 8 * hi + 8]
                w = pltpu.roll(w, (32 * (hi - k)) % 128, 1) if hi != k else w
                u = w if u is None else jnp.where(block == hi, w, u)
            u = u.astype(BF)
            own[i, k] = u
            vol[3 + i, 3 + k] = u

    def halo(n, ds, dt):
        i0, ni, i1 = halo_span(ds)
        k0, nk, k1 = halo_span(dt)
        return pltpu.make_async_remote_copy(
            src_ref=own.at[pl.ds(i0, ni), pl.ds(k0, nk)], dst_ref=vol.at[pl.ds(i1, ni), pl.ds(k1, nk)],
            send_sem=h_send.at[n], recv_sem=h_recv.at[n], device_id=(s + ds, t + dt), device_id_type=MESH)

    for n, (ds, dt) in enumerate(SIDES):
        @pl.when(there(ds, dt))
        def _():
            halo(n, ds, dt).start()

    def arrived(wanted):
        for n, (ds, dt) in enumerate(SIDES):
            if wanted(ds):
                @pl.when(there(-ds, -dt))
                def _():
                    halo(n, ds, dt).wait_recv()

    arrived(lambda ds: ds == 0)
    meanwhile()
    arrived(lambda ds: ds != 0)

    for r in near:
        z_go(r).wait_send()
    for q in range(nz):
        y_go(q).wait_send()
        for w in range(2):
            c_go(q, w).wait_send()
    p_go(0).wait_send()
    p_go(1).wait_send()
    for r in range(1, nx):
        x_go(r).wait_send()
        f_go(r, 0).wait_send()
        f_go(r, 1).wait_send()

    for n, (ds, dt) in enumerate(SIDES):
        @pl.when(there(ds, dt))
        def _():
            halo(n, ds, dt).wait_send()


def rolled(x, by):
    return pltpu.roll(x, by % 128, 1)


def conv_stages(ns, nt, u_ref, w1_ref, w2_ref, w3_ref, bias_ref, o_ref, z, act1, act2, fin):
    s, t = lax.axis_index("src"), lax.axis_index("tgt")
    lane = lax.broadcasted_iota(jnp.int32, (8, 128), 1)
    row = lax.broadcasted_iota(jnp.int32, (8, 128), 0)
    lane16 = lax.broadcasted_iota(jnp.int32, (16, 128), 1)
    first8, last8 = lane % 32 == 0, lane % 32 == 31
    first, last = lane16 % 32 == 0, lane16 % 32 == 31
    dot = functools.partial(jnp.dot, preferred_element_type=F32)

    def pieces(lo, hi):
        @pl.loop(lo, hi)
        def _(i):
            for k in range(10):
                u = u_ref[i, k].astype(F32)
                before = jnp.where(lane >= 32, rolled(u, 32), 0.0)
                after = jnp.where(lane < 96, rolled(u, -32), 0.0)
                for q, v in enumerate((jnp.where(row == 7, before, u), u, jnp.where(row == 0, after, u))):
                    left = jnp.where(first8, 0.0, rolled(v, 1))
                    right = jnp.where(last8, 0.0, rolled(v, -1))
                    own = (row - (3 * q - 1) + 8) % 8 <= 4
                    z[i, k, pl.ds(16 * q, 16)] = jnp.concatenate([
                        jnp.where(own, left, pltpu.roll(v, 5, 0)),
                        jnp.where(own, right, pltpu.roll(v, 2, 0))], 0).astype(BF)

    def put(act, i, k, j, v):
        act[i, k, 1 + j] = v.astype(BF)
        if j == 7:
            act[i, k, 0] = jnp.where(lane16 >= 32, rolled(v, 32), 0.0).astype(BF)
        if j == 0:
            act[i, k, 9] = jnp.where(lane16 < 96, rolled(v, -32), 0.0).astype(BF)

    def kept(i, k, off):
        gi, gk = 4 * s - off + i, 4 * t - off + k
        ok = (gi >= 0) & (gi < 4 * ns) & (gk >= 0) & (gk < 4 * nt)
        return jnp.where(ok, 1.0, 0.0)

    def layer_one(lo, hi):
        b1 = bias_ref[0]

        @pl.loop(lo, hi)
        def _(i):
            for kk in range(2):
                for q in range(3):
                    cols = []
                    for m in range(2):
                        cols.append(jnp.concatenate(
                            [z[i + a, 4 * kk + 2 * m + e, pl.ds(16 * q, 16)] for a in range(3) for e in range(4)], 0))
                    wide = 3 if q < 2 else 2
                    y = dot(w1_ref[pl.ds(96 * q, 32 * wide)], jnp.concatenate(cols, 1))
                    for m in range(2):
                        for dk in range(2):
                            k = 4 * kk + 2 * m + dk
                            keep = kept(i, k, 2)
                            for j in range(wide):
                                r = 32 * j + 16 * dk
                                v = jnp.maximum(y[r:r + 16, 128 * m:128 * m + 128] + b1, 0.0) * keep
                                put(act1, i, k, 3 * q + j, v)

    def rest():
        b2 = bias_ref[1]
        @pl.loop(0, 3)
        def _(ii):
            for kk in range(3):
                for p in range(4):
                    cols = []
                    for m in range(2):
                        cols.append(jnp.concatenate(
                            [act1[2 * ii + a, 2 * kk + e, 2 * p + m + b]
                             for a in range(4) for e in range(4) for b in range(3)], 0))
                    y = dot(w2_ref[...], jnp.concatenate(cols, 1))
                    for di in range(2):
                        for dk in range(2):
                            i, k = 2 * ii + di, 2 * kk + dk
                            keep = kept(i, k, 1)
                            r = 48 * (2 * di + dk)
                            for m in range(2):
                                h = slice(128 * m, 128 * m + 128)
                                v = (y[r + 16:r + 32, h] + jnp.where(first, 0.0, rolled(y[r:r + 16, h], 1))
                                     + jnp.where(last, 0.0, rolled(y[r + 32:r + 48, h], -1)) + b2)
                                put(act2, i, k, 2 * p + m, jnp.maximum(v, 0.0) * keep)

        w3 = w3_ref[...]
        b3 = bias_ref[2, pl.ds(0, 8)]
        for ii in range(2):
            for kk in range(2):
                per_col = []
                for q in range(5):
                    y = dot(w3, jnp.concatenate([jnp.concatenate(
                        [act2[2 * ii + a, 2 * kk + e, 2 * q + m] for a in range(4) for e in range(4)], 0)
                        for m in range(2)], 1))
                    per_col += [y[:, 0:128], y[:, 128:256]]
                buf = fin.at[2 * ii + kk]
                for j in range(8):
                    v = per_col[j][0:16] + per_col[j + 1][16:32] + per_col[j + 2][32:48]
                    left = pltpu.roll(jnp.where(first8, 0.0, rolled(v[0:8], 1)), 4, 0)
                    v = v[0:8] + left + jnp.where(last8, 0.0, rolled(v[8:16], -1)) + b3
                    buf[pl.ds(8 * j, 8)] = jnp.maximum(v, 0.0)
                for di in range(2):
                    for dk in range(2):
                        v = buf[pl.ds(2 * di + dk, 8, stride=8), :]
                        o_ref[2 * ii + di, 2 * kk + dk] = jnp.concatenate(
                            [v[:, 32 * q:32 * q + 32] for q in range(4)], 0).astype(BF)

    return pieces, layer_one, rest


def whole_kernel(ns, nt, *refs):
    given, (out, vol, w1, w2, w3, bias, z, act1, act2, fin), rest = refs[:8], refs[8:18], refs[18:]
    pieces, layer_one, others = conv_stages(ns, nt, vol, w1, w2, w3, bias, out, z, act1, act2, fin)

    def meanwhile():
        pieces(3, 7)
        layer_one(3, 5)

    volume_kernel(ns, nt, meanwhile, *given, vol, w1, w2, w3, bias, *rest)
    pieces(0, 3)
    pieces(7, 10)
    layer_one(0, 3)
    layer_one(5, 8)
    others()


def whole_call(ns, nt, *given):
    src, tgt = given[:2]
    hbm = pl.BlockSpec(memory_space=pl.ANY)
    vmem, dma = pltpu.VMEM, pltpu.SemaphoreType.DMA
    pairs = [nt // 4 - 1, nt // 4, nt // 2, ns // 2 - 1, 2, ns - 2, 8]
    return pl.pallas_call(
        functools.partial(whole_kernel, ns, nt),
        out_shape=pltpu.VMEM((4, 4, 32, 32), BF),
        in_specs=[hbm] * 7 + [pl.BlockSpec(memory_space=pltpu.SMEM)],
        out_specs=pl.BlockSpec(memory_space=pltpu.VMEM),
        scratch_shapes=[
            vmem((10, 10, 8, 128), BF), vmem((256, 192), BF), vmem((192, 768), BF), vmem((48, 256), BF),
            vmem((3, 16, 128), F32),
            vmem((10, 10, 48, 128), BF), vmem((8, 8, 10, 16, 128), BF), vmem((6, 6, 10, 16, 128), BF),
            vmem((4, 64, 128), F32),
            vmem(src.shape, BF), vmem((nt, src.shape[-1], 128), BF), vmem((ns, 128, tgt.shape[-1]), BF),
            vmem((4, 4, 8, 128), BF),
            vmem((27, 3, 16), BF), vmem((81, 16, 16), BF), vmem((27, 3, 16), BF), vmem((2, 1, 16), F32),
            vmem((128, 128), F32), vmem((128, 128), F32),
            dma((7,)),
        ] + [dma((max(n, 1),)) for n in pairs for _ in range(2)],
        compiler_params=pltpu.CompilerParams(
            collective_id=0, has_side_effects=True, vmem_limit_bytes=65000000),
    )(*given)


def solution(mesh):
    ns, nt = mesh.shape["src"], mesh.shape["tgt"]

    def local(source, target, conv_one, bias_one, conv_two, bias_two, conv_three, bias_three):
        out = whole_call(
            ns, nt, source.reshape(128, -1), target.reshape(128, -1),
            conv_one.reshape(27, 3, 16), bias_one.reshape(1, 16), conv_two.reshape(81, 16, 16),
            bias_two.reshape(1, 16), conv_three.reshape(27, 3, 16), bias_three.reshape(1, 1))
        return out[None]

    return jax.shard_map(
        local,
        mesh=mesh,
        in_specs=(P(None, "src", None, "tgt"), P(None, "tgt", None, "src")) + (P(),) * 6,
        out_specs=P(None, "src", "tgt", None, None),
        check_vma=False,
    )
```

```python
import functools

import jax
import jax.numpy as jnp
from jax import lax
from jax.experimental import pallas as pl
from jax.experimental.pallas import tpu as pltpu
from jax.sharding import PartitionSpec as P

F32, BF = jnp.float32, jnp.bfloat16

MESH = pl.DeviceIdType.MESH
EPS = 1e-6
SIDES = [(ds, dt) for ds in (-1, 0, 1) for dt in (-1, 0, 1) if ds or dt]
NT = (((1,), (1,)), ((), ()))


def halo_span(d):
    if d == 0:
        return 0, 4, 3
    return (1, 3, 0) if d > 0 else (0, 3, 7)


def iota(shape, dim):
    return lax.broadcasted_iota(jnp.int32, shape, dim)


def hot(mask):
    return jnp.where(mask, 1.0, 0.0).astype(BF)


def make_w1(c1, flat, w1):
    flat[...] = jnp.zeros_like(flat)
    for n in range(27):
        flat[pl.ds(3 * n, 3), pl.ds(0, 16)] = c1[n].astype(F32)
    xt = flat[...].T[0:16, 0:96].astype(BF)
    n = iota((1, 192), 1)
    a, across, half, at = n // 64, (n // 16) % 4, (n % 16) // 8, n % 8
    r = iota((96, 192), 0)
    for q in range(3):
        d = (at - (3 * q - 1) + 8) % 8
        from_ = jnp.where(d <= 4, d, jnp.where(half == 0, d - 5, d - 2))
        g = jnp.where(d <= 4, 2 * half, 1)
        for j in range(3 if q < 2 else 2):
            b = from_ - j
            for k in range(2):
                e = across - k
                inside = (from_ <= 4) & (b >= 0) & (b < 3) & (e >= 0) & (e < 3)
                key = jnp.where(inside, a * 27 + b * 9 + e * 3 + g, -1)
                w1[pl.ds(96 * q + 32 * j + 16 * k, 16)] = jnp.dot(
                    xt, hot(r == key), preferred_element_type=F32).astype(BF)


def make_w2(c2, w2):
    eye = hot(iota((16, 16), 0) == iota((16, 16), 1))
    none = jnp.zeros((16, 16), BF)
    for i in range(2):
        for k in range(2):
            for g in range(3):
                pieces = []
                for up in range(4):
                    for across in range(4):
                        for b in range(3):
                            a, e = up - i, across - k
                            inside = 0 <= a < 3 and 0 <= e < 3
                            pieces.append(c2[((a * 3 + b) * 3 + e) * 3 + g] if inside else none)
                w2[pl.ds(((2 * i + k) * 3 + g) * 16, 16)] = lax.dot_general(
                    eye, jnp.concatenate(pieces, 0), NT, preferred_element_type=F32).astype(BF)


def make_w3(c3, flat, w3):
    flat[...] = jnp.zeros_like(flat)
    for n in range(27):
        flat[pl.ds(3 * n, 3), pl.ds(0, 16)] = c3[n].astype(F32)
    y = flat[pl.ds(0, 96), pl.ds(0, 16)].astype(BF)
    wide = jnp.dot(y, hot(iota((16, 256), 1) % 16 == iota((16, 256), 0)), preferred_element_type=F32).astype(BF)
    m = iota((48, 1), 0)
    b, slot = m // 16, (m % 16) // 4
    g = jnp.where(slot == 0, 1, jnp.where(slot == 1, 0, 2))
    r = iota((48, 96), 1)
    mm, nn = iota((48, 256), 0), iota((48, 256), 1)
    up, across = nn // 64 - (mm // 2) % 2, (nn // 16) % 4 - mm % 2
    total = jnp.zeros((48, 256), F32)
    for a in range(3):
        for e in range(3):
            key = jnp.where(slot < 3, a * 27 + b * 9 + e * 3 + g, -1)
            part = jnp.dot(hot(r == key), wide, preferred_element_type=F32)
            total = total + jnp.where((up == a) & (across == e), part, 0.0)
    w3[...] = total.astype(BF)


def inverse_root(v):
    r = lax.rsqrt(v)
    return r * (1.5 - 0.5 * v * r * r)


def column(row):
    square = jnp.where(iota((16, 16), 0) == iota((16, 16), 1), jnp.broadcast_to(row, (16, 16)), 0.0)
    return jnp.broadcast_to(jnp.sum(square, axis=1, keepdims=True), (16, 128))


def volume_kernel(ns, nt, meanwhile, src_hbm, tgt_hbm, c1_hbm, b1_hbm, c2_hbm, b2_hbm, c3_hbm, b3_ref,
                  vol, w1, w2, w3, bias,
                  src, gs, gt, normed, own, c1, c2, c3, bs, flat1, flat3, load,
                  z_send, z_recv, y_send, y_recv, c_send, c_recv, x_send, x_recv, p_send, p_recv,
                  f_send, f_recv, h_send, h_recv):
    s, t = lax.axis_index("src"), lax.axis_index("tgt")
    nz, nx = nt // 4, ns // 2
    z, y, c = t // 4, (t // 2) % 2, t % 2
    x, h = s // 2, s % 2
    ch_s, ch_t = src.shape[-1], gt.shape[-1]

    fetches = [pltpu.make_async_copy(a, b, load.at[n]) for n, (a, b) in enumerate(
        [(src_hbm, src), (tgt_hbm, gt.at[s]), (c1_hbm, c1), (c2_hbm, c2), (c3_hbm, c3),
         (b1_hbm, bs.at[0]), (b2_hbm, bs.at[1])])]
    for f in fetches:
        f.start()

    vol[...] = jnp.zeros_like(vol)

    def tgt_at(zz, yy, cc):
        return 4 * zz + 2 * yy + cc

    def z_off(r):
        return lax.rem(z + r + nz, nz)

    def x_off(r):
        return lax.rem(x + r + nx, nx)

    def there(ds, dt):
        return (s + ds >= 0) & (s + ds < ns) & (t + dt >= 0) & (t + dt < nt)

    barrier = pltpu.get_barrier_semaphore()
    peers = [(s, tgt_at(z_off(r), y, c)) for r in range(1, nz)]
    peers += [(s, tgt_at(z, 1 - y, c)), (s, tgt_at(z, 1 - y, 1 - c)), (s, tgt_at(z, y, 1 - c))]
    peers += [(2 * x_off(r) + h, t) for r in range(1, nx)] + [(2 * x + 1 - h, t)]
    count = len(peers)
    for p in peers:
        pl.semaphore_signal(barrier, inc=1, device_id=p, device_id_type=MESH)
    for ds, dt in SIDES:
        count = count + jnp.where(there(ds, dt), 1, 0)

        @pl.when(there(ds, dt))
        def _():
            pl.semaphore_signal(barrier, inc=1, device_id=(s + ds, t + dt), device_id_type=MESH)

    fetches[0].wait()
    eye = hot(iota((ch_s, ch_s), 0) == iota((ch_s, ch_s), 1))
    gs[t] = lax.dot_general(eye, src[...], NT, preferred_element_type=F32).astype(BF)
    fetches[1].wait()
    pl.semaphore_wait(barrier, count)

    def remote(ref, sems, n, to):
        return pltpu.make_async_remote_copy(
            src_ref=ref, dst_ref=ref, send_sem=sems[0].at[n], recv_sem=sems[1].at[n],
            device_id=to, device_id_type=MESH)

    zs, ys, cs, xs, ps, fs = ((z_send, z_recv), (y_send, y_recv), (c_send, c_recv), (x_send, x_recv),
                              (p_send, p_recv), (f_send, f_recv))
    mate, twin, partner = (s, tgt_at(z, 1 - y, c)), (s, tgt_at(z, y, 1 - c)), (2 * x + 1 - h, t)
    across = (s, tgt_at(z, 1 - y, 1 - c))

    def z_go(r):
        return remote(gs.at[t], zs, r - 1, (s, tgt_at(z_off(r), y, c)))

    def z_come(r):
        return remote(gs.at[tgt_at(z_off(-r), y, c)], zs, r - 1, mate)

    def y_go(q):
        return remote(gs.at[tgt_at(z_off(-q), y, c)], ys, q, mate)

    def y_come(q):
        return remote(gs.at[tgt_at(z_off(-q), 1 - y, c)], ys, q, mate)

    def c_go(q, w):
        return remote(gs.at[tgt_at(z_off(-q), y, c)], cs, 2 * q + w, twin if w == 0 else across)

    def c_come(q, w):
        return remote(gs.at[tgt_at(z_off(-q), y if w == 0 else 1 - y, 1 - c)], cs, 2 * q + w, twin)

    def half(ref, m):
        return ref.at[pl.ds(64 * m, 64)]

    def x_go(r):
        return remote(gt.at[s], xs, r - 1, (2 * x_off(r) + h, t))

    def x_come(r):
        return remote(gt.at[2 * x_off(-r) + h], xs, r - 1, partner)

    def p_go(m):
        return remote(half(gt.at[s], m), ps, m, partner)

    def p_come(m):
        return remote(half(gt.at[2 * x + 1 - h], m), ps, m, partner)

    def f_go(r, m):
        return remote(half(gt.at[2 * x + 1 - h], m), fs, 2 * r - 2 + m, (2 * x_off(r) + h, t))

    def f_come(r, m):
        return remote(half(gt.at[2 * x_off(-r) + 1 - h], m), fs, 2 * r - 2 + m, partner)

    far = sorted(range(1, nx), key=lambda r: -min(r, nx - r))

    near = sorted(range(1, nz), key=lambda r: min(r, nz - r))
    for r in reversed(near):
        z_go(r).start()
    p_go(0).start()
    p_go(1).start()
    y_go(0).start()
    c_go(0, 1).start()
    for r in far:
        x_go(r).start()
    c_go(0, 0).start()

    for f in fetches[2:]:
        f.wait()
    make_w1(c1, flat1, w1)

    events = []
    for n, r in enumerate(near):
        d = min(r, nz - r)
        events.append((0.9 + 0.75 * d, "z", r))
    events += [(2.6, "p", 0), (2.8, "p", 1), (2.5, "w", 0), (3.6, "w", 1), (4.0, "w", 2)]
    for _, kind, q in sorted(events):
        if kind == "z":
            z_come(q).wait_recv()
            y_go(q).start()
            c_go(q, 1).start()
            c_go(q, 0).start()
        elif kind == "p":
            p_come(q).wait_recv()
            for r in far:
                f_go(r, q).start()
        elif q == 0:
            make_w3(c3, flat3, w3)
        elif q == 1:
            make_w2(c2, w2)
        else:
            bias[0] = column(bs[0])
            bias[1] = column(bs[1])
            bias[2] = jnp.full((16, 128), b3_ref[0, 0], F32)

    for q in range(nz):
        y_come(q).wait_recv()
        for w in range(2):
            c_come(q, w).wait_recv()
    sq = None
    for n in range(nt):
        v = gs[n].astype(F32)
        v = v * v
        for q in range(ch_s // 8):
            p = v[8 * q:8 * q + 8]
            sq = p if sq is None else sq + p
    inv_s = inverse_root(jnp.sum(sq, axis=0, keepdims=True) + EPS)
    per = ch_t // ch_s
    for n in range(ns):
        left = jnp.concatenate([gs[n * per + q] for q in range(per)], 0)
        normed[n] = (left.astype(F32) * inv_s).astype(BF)

    for r in range(1, nx):
        x_come(r).wait_recv()
    for r in range(1, nx):
        for m in range(2):
            f_come(r, m).wait_recv()
    sq = None
    for n in range(ns):
        v = gt[n].astype(F32)
        sq = v * v if sq is None else sq + v * v
    inv_t = inverse_root(jnp.sum(sq, axis=1, keepdims=True) + EPS)

    acc = jnp.zeros((128, 128), F32)
    for n in range(ns):
        right = (gt[n].astype(F32) * inv_t).astype(BF)
        acc = acc + jnp.dot(right, normed[n], preferred_element_type=F32)
    v = acc.T
    block = iota((8, 128), 1) // 32
    for i in range(4):
        for k in range(4):
            u = None
            for hi in range(4):
                w = v[32 * i + 8 * hi:32 * i + 8 * hi + 8]
                w = pltpu.roll(w, (32 * (hi - k)) % 128, 1) if hi != k else w
                u = w if u is None else jnp.where(block == hi, w, u)
            u = u.astype(BF)
            own[i, k] = u
            vol[3 + i, 3 + k] = u

    def halo(n, ds, dt):
        i0, ni, i1 = halo_span(ds)
        k0, nk, k1 = halo_span(dt)
        return pltpu.make_async_remote_copy(
            src_ref=own.at[pl.ds(i0, ni), pl.ds(k0, nk)], dst_ref=vol.at[pl.ds(i1, ni), pl.ds(k1, nk)],
            send_sem=h_send.at[n], recv_sem=h_recv.at[n], device_id=(s + ds, t + dt), device_id_type=MESH)

    for n, (ds, dt) in enumerate(SIDES):
        @pl.when(there(ds, dt))
        def _():
            halo(n, ds, dt).start()

    def arrived(wanted):
        for n, (ds, dt) in enumerate(SIDES):
            if wanted(ds):
                @pl.when(there(-ds, -dt))
                def _():
                    halo(n, ds, dt).wait_recv()

    arrived(lambda ds: ds == 0)
    meanwhile()
    arrived(lambda ds: ds != 0)

    for r in near:
        z_go(r).wait_send()
    for q in range(nz):
        y_go(q).wait_send()
        for w in range(2):
            c_go(q, w).wait_send()
    p_go(0).wait_send()
    p_go(1).wait_send()
    for r in range(1, nx):
        x_go(r).wait_send()
        f_go(r, 0).wait_send()
        f_go(r, 1).wait_send()

    for n, (ds, dt) in enumerate(SIDES):
        @pl.when(there(ds, dt))
        def _():
            halo(n, ds, dt).wait_send()


def rolled(x, by):
    return pltpu.roll(x, by % 128, 1)


def conv_stages(ns, nt, u_ref, w1_ref, w2_ref, w3_ref, bias_ref, o_ref, z, act1, act2, fin):
    s, t = lax.axis_index("src"), lax.axis_index("tgt")
    lane = lax.broadcasted_iota(jnp.int32, (8, 128), 1)
    row = lax.broadcasted_iota(jnp.int32, (8, 128), 0)
    lane16 = lax.broadcasted_iota(jnp.int32, (16, 128), 1)
    first8, last8 = lane % 32 == 0, lane % 32 == 31
    first, last = lane16 % 32 == 0, lane16 % 32 == 31
    dot = functools.partial(jnp.dot, preferred_element_type=F32)

    def pieces(lo, hi):
        @pl.loop(lo, hi)
        def _(i):
            for k in range(10):
                u = u_ref[i, k].astype(F32)
                before = jnp.where(lane >= 32, rolled(u, 32), 0.0)
                after = jnp.where(lane < 96, rolled(u, -32), 0.0)
                for q, v in enumerate((jnp.where(row == 7, before, u), u, jnp.where(row == 0, after, u))):
                    left = jnp.where(first8, 0.0, rolled(v, 1))
                    right = jnp.where(last8, 0.0, rolled(v, -1))
                    own = (row - (3 * q - 1) + 8) % 8 <= 4
                    z[i, k, pl.ds(16 * q, 16)] = jnp.concatenate([
                        jnp.where(own, left, pltpu.roll(v, 5, 0)),
                        jnp.where(own, right, pltpu.roll(v, 2, 0))], 0).astype(BF)

    def put(act, i, k, j, v):
        act[i, k, 1 + j] = v.astype(BF)
        if j == 7:
            act[i, k, 0] = jnp.where(lane16 >= 32, rolled(v, 32), 0.0).astype(BF)
        if j == 0:
            act[i, k, 9] = jnp.where(lane16 < 96, rolled(v, -32), 0.0).astype(BF)

    def kept(i, k, off):
        gi, gk = 4 * s - off + i, 4 * t - off + k
        ok = (gi >= 0) & (gi < 4 * ns) & (gk >= 0) & (gk < 4 * nt)
        return jnp.where(ok, 1.0, 0.0)

    def layer_one(lo, hi):
        b1 = bias_ref[0]

        for i in range(lo, hi):
            for kk in range(2):
                for q in range(3):
                    cols = []
                    for m in range(2):
                        cols.append(jnp.concatenate(
                            [z[i + a, 4 * kk + 2 * m + e, pl.ds(16 * q, 16)] for a in range(3) for e in range(4)], 0))
                    wide = 3 if q < 2 else 2
                    y = dot(w1_ref[pl.ds(96 * q, 32 * wide)], jnp.concatenate(cols, 1))
                    for m in range(2):
                        for dk in range(2):
                            k = 4 * kk + 2 * m + dk
                            keep = kept(i, k, 2)
                            for j in range(wide):
                                r = 32 * j + 16 * dk
                                v = jnp.maximum(y[r:r + 16, 128 * m:128 * m + 128] + b1, 0.0) * keep
                                put(act1, i, k, 3 * q + j, v)

    def rest():
        b2 = bias_ref[1]
        for ii in range(3):
            for kk in range(3):
                for p in range(4):
                    cols = []
                    for m in range(2):
                        cols.append(jnp.concatenate(
                            [act1[2 * ii + a, 2 * kk + e, 2 * p + m + b]
                             for a in range(4) for e in range(4) for b in range(3)], 0))
                    y = dot(w2_ref[...], jnp.concatenate(cols, 1))
                    for di in range(2):
                        for dk in range(2):
                            i, k = 2 * ii + di, 2 * kk + dk
                            keep = kept(i, k, 1)
                            r = 48 * (2 * di + dk)
                            for m in range(2):
                                h = slice(128 * m, 128 * m + 128)
                                v = (y[r + 16:r + 32, h] + jnp.where(first, 0.0, rolled(y[r:r + 16, h], 1))
                                     + jnp.where(last, 0.0, rolled(y[r + 32:r + 48, h], -1)) + b2)
                                put(act2, i, k, 2 * p + m, jnp.maximum(v, 0.0) * keep)

        w3 = w3_ref[...]
        b3 = bias_ref[2, pl.ds(0, 8)]
        for ii in range(2):
            for kk in range(2):
                per_col = []
                for q in range(5):
                    y = dot(w3, jnp.concatenate([jnp.concatenate(
                        [act2[2 * ii + a, 2 * kk + e, 2 * q + m] for a in range(4) for e in range(4)], 0)
                        for m in range(2)], 1))
                    per_col += [y[:, 0:128], y[:, 128:256]]
                buf = fin.at[2 * ii + kk]
                for j in range(8):
                    v = per_col[j][0:16] + per_col[j + 1][16:32] + per_col[j + 2][32:48]
                    left = pltpu.roll(jnp.where(first8, 0.0, rolled(v[0:8], 1)), 4, 0)
                    v = v[0:8] + left + jnp.where(last8, 0.0, rolled(v[8:16], -1)) + b3
                    buf[pl.ds(8 * j, 8)] = jnp.maximum(v, 0.0)
                for di in range(2):
                    for dk in range(2):
                        v = buf[pl.ds(2 * di + dk, 8, stride=8), :]
                        o_ref[2 * ii + di, 2 * kk + dk] = jnp.concatenate(
                            [v[:, 32 * q:32 * q + 32] for q in range(4)], 0).astype(BF)

    return pieces, layer_one, rest


def whole_kernel(ns, nt, *refs):
    given, (out, vol, w1, w2, w3, bias, z, act1, act2, fin), rest = refs[:8], refs[8:18], refs[18:]
    pieces, layer_one, others = conv_stages(ns, nt, vol, w1, w2, w3, bias, out, z, act1, act2, fin)

    def meanwhile():
        pieces(3, 7)
        layer_one(3, 5)

    volume_kernel(ns, nt, meanwhile, *given, vol, w1, w2, w3, bias, *rest)
    pieces(0, 3)
    pieces(7, 10)
    layer_one(0, 3)
    layer_one(5, 8)
    others()


def whole_call(ns, nt, *given):
    src, tgt = given[:2]
    hbm = pl.BlockSpec(memory_space=pl.ANY)
    vmem, dma = pltpu.VMEM, pltpu.SemaphoreType.DMA
    pairs = [nt // 4 - 1, nt // 4, nt // 2, ns // 2 - 1, 2, ns - 2, 8]
    return pl.pallas_call(
        functools.partial(whole_kernel, ns, nt),
        out_shape=pltpu.VMEM((4, 4, 32, 32), BF),
        in_specs=[hbm] * 7 + [pl.BlockSpec(memory_space=pltpu.SMEM)],
        out_specs=pl.BlockSpec(memory_space=pltpu.VMEM),
        scratch_shapes=[
            vmem((10, 10, 8, 128), BF), vmem((256, 192), BF), vmem((192, 768), BF), vmem((48, 256), BF),
            vmem((3, 16, 128), F32),
            vmem((10, 10, 48, 128), BF), vmem((8, 8, 10, 16, 128), BF), vmem((6, 6, 10, 16, 128), BF),
            vmem((4, 64, 128), F32),
            vmem(src.shape, BF), vmem((nt, src.shape[-1], 128), BF), vmem((ns, 128, tgt.shape[-1]), BF),
            vmem((ns, 128, tgt.shape[-1]), BF),
            vmem((4, 4, 8, 128), BF),
            vmem((27, 3, 16), BF), vmem((81, 16, 16), BF), vmem((27, 3, 16), BF), vmem((2, 1, 16), F32),
            vmem((128, 128), F32), vmem((128, 128), F32),
            dma((7,)),
        ] + [dma((max(n, 1),)) for n in pairs for _ in range(2)],
        compiler_params=pltpu.CompilerParams(
            collective_id=0, has_side_effects=True, vmem_limit_bytes=65000000),
    )(*given)


def solution(mesh):
    ns, nt = mesh.shape["src"], mesh.shape["tgt"]

    def local(source, target, conv_one, bias_one, conv_two, bias_two, conv_three, bias_three):
        out = whole_call(
            ns, nt, source.reshape(128, -1), target.reshape(128, -1),
            conv_one.reshape(27, 3, 16), bias_one.reshape(1, 16), conv_two.reshape(81, 16, 16),
            bias_two.reshape(1, 16), conv_three.reshape(27, 3, 16), bias_three.reshape(1, 1))
        return out[None]

    return jax.shard_map(
        local,
        mesh=mesh,
        in_specs=(P(None, "src", None, "tgt"), P(None, "tgt", None, "src")) + (P(),) * 6,
        out_specs=P(None, "src", "tgt", None, None),
        check_vma=False,
    )
```

```python
import functools

import jax
import jax.numpy as jnp
from jax import lax
from jax.experimental import pallas as pl
from jax.experimental.pallas import tpu as pltpu
from jax.sharding import PartitionSpec as P

F32, BF = jnp.float32, jnp.bfloat16

MESH = pl.DeviceIdType.MESH
EPS = 1e-6
SIDES = [(ds, dt) for ds in (-1, 0, 1) for dt in (-1, 0, 1) if ds or dt]
NT = (((1,), (1,)), ((), ()))


def halo_span(d):
    if d == 0:
        return 0, 4, 3
    return (1, 3, 0) if d > 0 else (0, 3, 7)


def iota(shape, dim):
    return lax.broadcasted_iota(jnp.int32, shape, dim)


def hot(mask):
    return jnp.where(mask, 1.0, 0.0).astype(BF)


def make_w1(c1, flat, w1):
    flat[...] = jnp.zeros_like(flat)
    for n in range(27):
        flat[pl.ds(3 * n, 3), pl.ds(0, 16)] = c1[n].astype(F32)
    xt = flat[...].T[0:16, 0:96].astype(BF)
    n = iota((1, 192), 1)
    a, across, half, at = n // 64, (n // 16) % 4, (n % 16) // 8, n % 8
    r = iota((96, 192), 0)
    for q in range(3):
        d = (at - (3 * q - 1) + 8) % 8
        from_ = jnp.where(d <= 4, d, jnp.where(half == 0, d - 5, d - 2))
        g = jnp.where(d <= 4, 2 * half, 1)
        for j in range(3 if q < 2 else 2):
            b = from_ - j
            for k in range(2):
                e = across - k
                inside = (from_ <= 4) & (b >= 0) & (b < 3) & (e >= 0) & (e < 3)
                key = jnp.where(inside, a * 27 + b * 9 + e * 3 + g, -1)
                w1[pl.ds(96 * q + 32 * j + 16 * k, 16)] = jnp.dot(
                    xt, hot(r == key), preferred_element_type=F32).astype(BF)


def make_w2(c2, w2):
    eye = hot(iota((16, 16), 0) == iota((16, 16), 1))
    none = jnp.zeros((16, 16), BF)
    for i in range(2):
        for k in range(2):
            for g in range(3):
                pieces = []
                for up in range(4):
                    for across in range(4):
                        for b in range(3):
                            a, e = up - i, across - k
                            inside = 0 <= a < 3 and 0 <= e < 3
                            pieces.append(c2[((a * 3 + b) * 3 + e) * 3 + g] if inside else none)
                w2[pl.ds(((2 * i + k) * 3 + g) * 16, 16)] = lax.dot_general(
                    eye, jnp.concatenate(pieces, 0), NT, preferred_element_type=F32).astype(BF)


def make_w3(c3, flat, w3):
    flat[...] = jnp.zeros_like(flat)
    for n in range(27):
        flat[pl.ds(3 * n, 3), pl.ds(0, 16)] = c3[n].astype(F32)
    y = flat[pl.ds(0, 96), pl.ds(0, 16)].astype(BF)
    wide = jnp.dot(y, hot(iota((16, 256), 1) % 16 == iota((16, 256), 0)), preferred_element_type=F32).astype(BF)
    m = iota((48, 1), 0)
    b, slot = m // 16, (m % 16) // 4
    g = jnp.where(slot == 0, 1, jnp.where(slot == 1, 0, 2))
    r = iota((48, 96), 1)
    mm, nn = iota((48, 256), 0), iota((48, 256), 1)
    up, across = nn // 64 - (mm // 2) % 2, (nn // 16) % 4 - mm % 2
    total = jnp.zeros((48, 256), F32)
    for a in range(3):
        for e in range(3):
            key = jnp.where(slot < 3, a * 27 + b * 9 + e * 3 + g, -1)
            part = jnp.dot(hot(r == key), wide, preferred_element_type=F32)
            total = total + jnp.where((up == a) & (across == e), part, 0.0)
    w3[...] = total.astype(BF)


def inverse_root(v):
    r = lax.rsqrt(v)
    return r * (1.5 - 0.5 * v * r * r)


def column(row):
    square = jnp.where(iota((16, 16), 0) == iota((16, 16), 1), jnp.broadcast_to(row, (16, 16)), 0.0)
    return jnp.broadcast_to(jnp.sum(square, axis=1, keepdims=True), (16, 128))


def volume_kernel(ns, nt, meanwhile, src_hbm, tgt_hbm, c1_hbm, b1_hbm, c2_hbm, b2_hbm, c3_hbm, b3_ref,
                  vol, w1, w2, w3, bias,
                  src, gs, gt, normed, own, c1, c2, c3, bs, flat1, flat3, load,
                  z_send, z_recv, y_send, y_recv, c_send, c_recv, x_send, x_recv, p_send, p_recv,
                  f_send, f_recv, h_send, h_recv):
    s, t = lax.axis_index("src"), lax.axis_index("tgt")
    nz, nx = nt // 4, ns // 2
    z, y, c = t // 4, (t // 2) % 2, t % 2
    x, h = s // 2, s % 2
    ch_s, ch_t = src.shape[-1], gt.shape[-1]

    fetches = [pltpu.make_async_copy(a, b, load.at[n]) for n, (a, b) in enumerate(
        [(src_hbm, src), (tgt_hbm, gt.at[s]), (c1_hbm, c1), (c2_hbm, c2), (c3_hbm, c3),
         (b1_hbm, bs.at[0]), (b2_hbm, bs.at[1])])]
    for f in fetches:
        f.start()

    vol[...] = jnp.zeros_like(vol)

    def tgt_at(zz, yy, cc):
        return 4 * zz + 2 * yy + cc

    def z_off(r):
        return lax.rem(z + r + nz, nz)

    def x_off(r):
        return lax.rem(x + r + nx, nx)

    def there(ds, dt):
        return (s + ds >= 0) & (s + ds < ns) & (t + dt >= 0) & (t + dt < nt)

    barrier = pltpu.get_barrier_semaphore()
    peers = [(s, tgt_at(z_off(r), y, c)) for r in range(1, nz)]
    peers += [(s, tgt_at(z, 1 - y, c)), (s, tgt_at(z, 1 - y, 1 - c)), (s, tgt_at(z, y, 1 - c))]
    peers += [(2 * x_off(r) + h, t) for r in range(1, nx)] + [(2 * x + 1 - h, t)]
    count = len(peers)
    for p in peers:
        pl.semaphore_signal(barrier, inc=1, device_id=p, device_id_type=MESH)
    for ds, dt in SIDES:
        count = count + jnp.where(there(ds, dt), 1, 0)

        @pl.when(there(ds, dt))
        def _():
            pl.semaphore_signal(barrier, inc=1, device_id=(s + ds, t + dt), device_id_type=MESH)

    fetches[0].wait()
    eye = hot(iota((ch_s, ch_s), 0) == iota((ch_s, ch_s), 1))
    gs[t] = lax.dot_general(eye, src[...], NT, preferred_element_type=F32).astype(BF)
    fetches[1].wait()
    pl.semaphore_wait(barrier, count)

    def remote(ref, sems, n, to):
        return pltpu.make_async_remote_copy(
            src_ref=ref, dst_ref=ref, send_sem=sems[0].at[n], recv_sem=sems[1].at[n],
            device_id=to, device_id_type=MESH)

    zs, ys, cs, xs, ps, fs = ((z_send, z_recv), (y_send, y_recv), (c_send, c_recv), (x_send, x_recv),
                              (p_send, p_recv), (f_send, f_recv))
    mate, twin, partner = (s, tgt_at(z, 1 - y, c)), (s, tgt_at(z, y, 1 - c)), (2 * x + 1 - h, t)
    across = (s, tgt_at(z, 1 - y, 1 - c))

    def z_go(r):
        return remote(gs.at[t], zs, r - 1, (s, tgt_at(z_off(r), y, c)))

    def z_come(r):
        return remote(gs.at[tgt_at(z_off(-r), y, c)], zs, r - 1, mate)

    def y_go(q):
        return remote(gs.at[tgt_at(z_off(-q), y, c)], ys, q, mate)

    def y_come(q):
        return remote(gs.at[tgt_at(z_off(-q), 1 - y, c)], ys, q, mate)

    def c_go(q, w):
        return remote(gs.at[tgt_at(z_off(-q), y, c)], cs, 2 * q + w, twin if w == 0 else across)

    def c_come(q, w):
        return remote(gs.at[tgt_at(z_off(-q), y if w == 0 else 1 - y, 1 - c)], cs, 2 * q + w, twin)

    def half(ref, m):
        return ref.at[pl.ds(64 * m, 64)]

    def x_go(r):
        return remote(gt.at[s], xs, r - 1, (2 * x_off(r) + h, t))

    def x_come(r):
        return remote(gt.at[2 * x_off(-r) + h], xs, r - 1, partner)

    def p_go(m):
        return remote(half(gt.at[s], m), ps, m, partner)

    def p_come(m):
        return remote(half(gt.at[2 * x + 1 - h], m), ps, m, partner)

    def f_go(r, m):
        return remote(half(gt.at[2 * x + 1 - h], m), fs, 2 * r - 2 + m, (2 * x_off(r) + h, t))

    def f_come(r, m):
        return remote(half(gt.at[2 * x_off(-r) + 1 - h], m), fs, 2 * r - 2 + m, partner)

    far = sorted(range(1, nx), key=lambda r: -min(r, nx - r))

    near = sorted(range(1, nz), key=lambda r: min(r, nz - r))
    for r in reversed(near):
        z_go(r).start()
    p_go(0).start()
    p_go(1).start()
    y_go(0).start()
    c_go(0, 1).start()
    for r in far:
        x_go(r).start()
    c_go(0, 0).start()

    for f in fetches[2:]:
        f.wait()
    make_w1(c1, flat1, w1)

    events = []
    for n, r in enumerate(near):
        d = min(r, nz - r)
        events.append((0.9 + 0.75 * d, "z", r))
    events += [(2.6, "p", 0), (2.8, "p", 1), (2.5, "w", 0), (3.6, "w", 1), (4.0, "w", 2)]
    for _, kind, q in sorted(events):
        if kind == "z":
            z_come(q).wait_recv()
            y_go(q).start()
            c_go(q, 1).start()
            c_go(q, 0).start()
        elif kind == "p":
            p_come(q).wait_recv()
            for r in far:
                f_go(r, q).start()
        elif q == 0:
            make_w3(c3, flat3, w3)
        elif q == 1:
            make_w2(c2, w2)
        else:
            bias[0] = column(bs[0])
            bias[1] = column(bs[1])
            bias[2] = jnp.full((16, 128), b3_ref[0, 0], F32)

    for q in range(nz):
        y_come(q).wait_recv()
        for w in range(2):
            c_come(q, w).wait_recv()
    sq = None
    for n in range(nt):
        v = gs[n].astype(F32)
        v = v * v
        for q in range(ch_s // 8):
            p = v[8 * q:8 * q + 8]
            sq = p if sq is None else sq + p
    inv_s = inverse_root(jnp.sum(sq, axis=0, keepdims=True) + EPS)
    per = ch_t // ch_s
    for n in range(ns):
        left = jnp.concatenate([gs[n * per + q] for q in range(per)], 0)
        normed[n] = (left.astype(F32) * inv_s).astype(BF)

    for r in range(1, nx):
        x_come(r).wait_recv()
    for r in range(1, nx):
        for m in range(2):
            f_come(r, m).wait_recv()
    sq = None
    for n in range(ns):
        v = gt[n].astype(F32)
        sq = v * v if sq is None else sq + v * v
    inv_t = inverse_root(jnp.sum(sq, axis=1, keepdims=True) + EPS)

    acc = jnp.zeros((128, 128), F32)
    for n in range(ns):
        right = (gt[n].astype(F32) * inv_t).astype(BF)
        acc = acc + jnp.dot(right, normed[n], preferred_element_type=F32)
    v = acc.T
    block = iota((8, 128), 1) // 32
    for i in range(4):
        for k in range(4):
            u = None
            for hi in range(4):
                w = v[32 * i + 8 * hi:32 * i + 8 * hi + 8]
                w = pltpu.roll(w, (32 * (hi - k)) % 128, 1) if hi != k else w
                u = w if u is None else jnp.where(block == hi, w, u)
            u = u.astype(BF)
            own[i, k] = u
            vol[3 + i, 3 + k] = u

    def halo(n, ds, dt):
        i0, ni, i1 = halo_span(ds)
        k0, nk, k1 = halo_span(dt)
        return pltpu.make_async_remote_copy(
            src_ref=own.at[pl.ds(i0, ni), pl.ds(k0, nk)], dst_ref=vol.at[pl.ds(i1, ni), pl.ds(k1, nk)],
            send_sem=h_send.at[n], recv_sem=h_recv.at[n], device_id=(s + ds, t + dt), device_id_type=MESH)

    for n, (ds, dt) in enumerate(SIDES):
        @pl.when(there(ds, dt))
        def _():
            halo(n, ds, dt).start()

    def arrived(wanted):
        for n, (ds, dt) in enumerate(SIDES):
            if wanted(ds):
                @pl.when(there(-ds, -dt))
                def _():
                    halo(n, ds, dt).wait_recv()

    arrived(lambda ds: ds == 0)
    meanwhile()
    arrived(lambda ds: ds != 0)

    for r in near:
        z_go(r).wait_send()
    for q in range(nz):
        y_go(q).wait_send()
        for w in range(2):
            c_go(q, w).wait_send()
    p_go(0).wait_send()
    p_go(1).wait_send()
    for r in range(1, nx):
        x_go(r).wait_send()
        f_go(r, 0).wait_send()
        f_go(r, 1).wait_send()

    for n, (ds, dt) in enumerate(SIDES):
        @pl.when(there(ds, dt))
        def _():
            halo(n, ds, dt).wait_send()


def rolled(x, by):
    return pltpu.roll(x, by % 128, 1)


def conv_stages(ns, nt, u_ref, w1_ref, w2_ref, w3_ref, bias_ref, o_ref, z, act1, act2, fin):
    s, t = lax.axis_index("src"), lax.axis_index("tgt")
    lane = lax.broadcasted_iota(jnp.int32, (8, 128), 1)
    row = lax.broadcasted_iota(jnp.int32, (8, 128), 0)
    lane16 = lax.broadcasted_iota(jnp.int32, (16, 128), 1)
    first8, last8 = lane % 32 == 0, lane % 32 == 31
    first, last = lane16 % 32 == 0, lane16 % 32 == 31
    dot = functools.partial(jnp.dot, preferred_element_type=F32)

    def pieces(lo, hi):
        for i in range(lo, hi):
            for k in range(10):
                u = u_ref[i, k].astype(F32)
                before = jnp.where(lane >= 32, rolled(u, 32), 0.0)
                after = jnp.where(lane < 96, rolled(u, -32), 0.0)
                for q, v in enumerate((jnp.where(row == 7, before, u), u, jnp.where(row == 0, after, u))):
                    left = jnp.where(first8, 0.0, rolled(v, 1))
                    right = jnp.where(last8, 0.0, rolled(v, -1))
                    own = (row - (3 * q - 1) + 8) % 8 <= 4
                    z[i, k, pl.ds(16 * q, 16)] = jnp.concatenate([
                        jnp.where(own, left, pltpu.roll(v, 5, 0)),
                        jnp.where(own, right, pltpu.roll(v, 2, 0))], 0).astype(BF)

    def put(act, i, k, j, v):
        act[i, k, 1 + j] = v.astype(BF)
        if j == 7:
            act[i, k, 0] = jnp.where(lane16 >= 32, rolled(v, 32), 0.0).astype(BF)
        if j == 0:
            act[i, k, 9] = jnp.where(lane16 < 96, rolled(v, -32), 0.0).astype(BF)

    def kept(i, k, off):
        gi, gk = 4 * s - off + i, 4 * t - off + k
        ok = (gi >= 0) & (gi < 4 * ns) & (gk >= 0) & (gk < 4 * nt)
        return jnp.where(ok, 1.0, 0.0)

    def layer_one(lo, hi):
        b1 = bias_ref[0]

        for i in range(lo, hi):
            for kk in range(2):
                for q in range(3):
                    cols = []
                    for m in range(2):
                        cols.append(jnp.concatenate(
                            [z[i + a, 4 * kk + 2 * m + e, pl.ds(16 * q, 16)] for a in range(3) for e in range(4)], 0))
                    wide = 3 if q < 2 else 2
                    y = dot(w1_ref[pl.ds(96 * q, 32 * wide)], jnp.concatenate(cols, 1))
                    for m in range(2):
                        for dk in range(2):
                            k = 4 * kk + 2 * m + dk
                            keep = kept(i, k, 2)
                            for j in range(wide):
                                r = 32 * j + 16 * dk
                                v = jnp.maximum(y[r:r + 16, 128 * m:128 * m + 128] + b1, 0.0) * keep
                                put(act1, i, k, 3 * q + j, v)

    def rest():
        b2 = bias_ref[1]
        for ii in range(3):
            for kk in range(3):
                for p in range(4):
                    cols = []
                    for m in range(2):
                        cols.append(jnp.concatenate(
                            [act1[2 * ii + a, 2 * kk + e, 2 * p + m + b]
                             for a in range(4) for e in range(4) for b in range(3)], 0))
                    y = dot(w2_ref[...], jnp.concatenate(cols, 1))
                    for di in range(2):
                        for dk in range(2):
                            i, k = 2 * ii + di, 2 * kk + dk
                            keep = kept(i, k, 1)
                            r = 48 * (2 * di + dk)
                            for m in range(2):
                                h = slice(128 * m, 128 * m + 128)
                                v = (y[r + 16:r + 32, h] + jnp.where(first, 0.0, rolled(y[r:r + 16, h], 1))
                                     + jnp.where(last, 0.0, rolled(y[r + 32:r + 48, h], -1)) + b2)
                                put(act2, i, k, 2 * p + m, jnp.maximum(v, 0.0) * keep)

        w3 = w3_ref[...]
        b3 = bias_ref[2, pl.ds(0, 8)]
        for ii in range(2):
            for kk in range(2):
                per_col = []
                for q in range(5):
                    y = dot(w3, jnp.concatenate([jnp.concatenate(
                        [act2[2 * ii + a, 2 * kk + e, 2 * q + m] for a in range(4) for e in range(4)], 0)
                        for m in range(2)], 1))
                    per_col += [y[:, 0:128], y[:, 128:256]]
                buf = fin.at[2 * ii + kk]
                for j in range(8):
                    v = per_col[j][0:16] + per_col[j + 1][16:32] + per_col[j + 2][32:48]
                    left = pltpu.roll(jnp.where(first8, 0.0, rolled(v[0:8], 1)), 4, 0)
                    v = v[0:8] + left + jnp.where(last8, 0.0, rolled(v[8:16], -1)) + b3
                    buf[pl.ds(8 * j, 8)] = jnp.maximum(v, 0.0)
                for di in range(2):
                    for dk in range(2):
                        v = buf[pl.ds(2 * di + dk, 8, stride=8), :]
                        o_ref[2 * ii + di, 2 * kk + dk] = jnp.concatenate(
                            [v[:, 32 * q:32 * q + 32] for q in range(4)], 0).astype(BF)

    return pieces, layer_one, rest


def whole_kernel(ns, nt, *refs):
    given, (out, vol, w1, w2, w3, bias, z, act1, act2, fin), rest = refs[:8], refs[8:18], refs[18:]
    pieces, layer_one, others = conv_stages(ns, nt, vol, w1, w2, w3, bias, out, z, act1, act2, fin)

    def meanwhile():
        pieces(3, 7)
        layer_one(3, 5)

    volume_kernel(ns, nt, meanwhile, *given, vol, w1, w2, w3, bias, *rest)
    pieces(0, 3)
    pieces(7, 10)
    layer_one(0, 3)
    layer_one(5, 8)
    others()


def whole_call(ns, nt, *given):
    src, tgt = given[:2]
    hbm = pl.BlockSpec(memory_space=pl.ANY)
    vmem, dma = pltpu.VMEM, pltpu.SemaphoreType.DMA
    pairs = [nt // 4 - 1, nt // 4, nt // 2, ns // 2 - 1, 2, ns - 2, 8]
    return pl.pallas_call(
        functools.partial(whole_kernel, ns, nt),
        out_shape=pltpu.VMEM((4, 4, 32, 32), BF),
        in_specs=[hbm] * 7 + [pl.BlockSpec(memory_space=pltpu.SMEM)],
        out_specs=pl.BlockSpec(memory_space=pltpu.VMEM),
        scratch_shapes=[
            vmem((10, 10, 8, 128), BF), vmem((256, 192), BF), vmem((192, 768), BF), vmem((48, 256), BF),
            vmem((3, 16, 128), F32),
            vmem((10, 10, 48, 128), BF), vmem((8, 8, 10, 16, 128), BF), vmem((6, 6, 10, 16, 128), BF),
            vmem((4, 64, 128), F32),
            vmem(src.shape, BF), vmem((nt, src.shape[-1], 128), BF), vmem((ns, 128, tgt.shape[-1]), BF),
            vmem((ns, 128, tgt.shape[-1]), BF),
            vmem((4, 4, 8, 128), BF),
            vmem((27, 3, 16), BF), vmem((81, 16, 16), BF), vmem((27, 3, 16), BF), vmem((2, 1, 16), F32),
            vmem((128, 128), F32), vmem((128, 128), F32),
            dma((7,)),
        ] + [dma((max(n, 1),)) for n in pairs for _ in range(2)],
        compiler_params=pltpu.CompilerParams(
            collective_id=0, has_side_effects=True, vmem_limit_bytes=65000000),
    )(*given)


def solution(mesh):
    ns, nt = mesh.shape["src"], mesh.shape["tgt"]

    def local(source, target, conv_one, bias_one, conv_two, bias_two, conv_three, bias_three):
        out = whole_call(
            ns, nt, source.reshape(128, -1), target.reshape(128, -1),
            conv_one.reshape(27, 3, 16), bias_one.reshape(1, 16), conv_two.reshape(81, 16, 16),
            bias_two.reshape(1, 16), conv_three.reshape(27, 3, 16), bias_three.reshape(1, 1))
        return out[None]

    return jax.shard_map(
        local,
        mesh=mesh,
        in_specs=(P(None, "src", None, "tgt"), P(None, "tgt", None, "src")) + (P(),) * 6,
        out_specs=P(None, "src", "tgt", None, None),
        check_vma=False,
    )
```
